128 devices in a mesh: dp: 64 (over y, z_lo, x, core), seq: 2 (over z_hi).
Axes of the slice: x: 4, y: 4, z: 4 (z_hi: 2, z_lo: 2; z = z_hi * 2 + z_lo), core: 2. Of those that a mesh axis runs over, the one named last changes fastest.
Arguments:
- hidden_in: bfloat16 [65536, 2048], P(('dp', 'seq')), may hold values from -6 to 6
- norm_gain: float32 [2048], replicated, may hold values from 0.1 to 1.9
- w_qk: bfloat16 [2048, 3072], P(('dp', 'seq')), may hold values from -1 to 1
- w_v: bfloat16 [2048, 1024], P(('dp', 'seq')), may hold values from -0.125 to 0.125
- w_o: bfloat16 [2048, 2048], P(('dp', 'seq')), may hold values from -0.125 to 0.125
- prompt_pages: int32 [64], replicated, may hold values from 1 to 17, 512 in all
- last_fill: int32 [64], replicated, may hold values from 1 to 128
- page_slots: int32 [512], P('dp'), may hold values from 0 to 7, as said below
Outputs:
- attended: bfloat16 [65536, 2048], P(('dp', 'seq'))
- key_cache: bfloat16 [512, 128, 1024], P(('dp', 'seq'))
- value_cache: bfloat16 [512, 128, 1024], P(('dp', 'seq'))
The draws below stay inside these ranges and needn't reach their ends.
Inputs may be any that keep to these rules, and one draw needn't show every extreme that they name: `prompt_pages`: the prompts' pages lie end to end from position 0 and add up to 512. `page_slots`: each aligned run of 8 entries is a permutation of 0 to 7.
All inputs are finite; a program needn't handle non-finite values.
Results may differ from the reference program's by a relative error of at most 0.01.
The reference program's roundings to bfloat16 on the way (of `normed`, `queries`, `keys`, `values`, `weights` and `attn`) count: a program that leaves them out, or rounds other values in their place, can miss the bound.
Values may be sent and summed in bfloat16 or wider, within the bound.
No kernel may reach another device: no remote copies, remote signals or barrier semaphores. Data moves between devices by JAX's collectives and lax.ppermute only.
A program may use at most 192 MiB of HBM per device.

```python
import math
import jax
import jax.numpy as jnp
import numpy as np
from jax import lax

D = 2048
HEADS = 16
KV_HEADS = 8
HEAD_DIM = 128
TOK_DEV = 512
PAGE = 128
REACH = 4
MAXPG = 17
TOKENS = 65536
NPAGES = 512
NREQ = 64
GROUP_PAGES = 8


def draw_w_qk(key, part):
    columns = (HEADS + KV_HEADS) * HEAD_DIM
    base = jax.random.truncated_normal(key, -4.0, 4.0, (D, columns), jnp.float32) / math.sqrt(D)
    return jnp.clip(base, -1.0, 1.0).astype(jnp.bfloat16)


def draw_page_slots(key, part):
    groups = NPAGES // GROUP_PAGES
    group_keys = jax.random.split(jax.random.fold_in(key, 3), groups)
    orders = jax.vmap(lambda single: jax.random.permutation(single, GROUP_PAGES))(group_keys)
    return orders.reshape(NPAGES).astype(jnp.int32)


def place_ends(drawn, rng, smallest, top_value):
    index_at = [jax.random.randint(jax.random.fold_in(rng, axis), (), 0, length) for axis, length in enumerate(drawn.shape)]
    longest = drawn.shape.index(max(drawn.shape))
    next_to = index_at[:longest] + [(index_at[longest] + 1) % drawn.shape[longest]] + index_at[longest + 1:]
    return drawn.at[tuple(index_at)].set(smallest).at[tuple(next_to)].set(top_value)


def level_of(key, dims, pieces, smallest, top_value):
    level = 1.0
    for dim, blocks in pieces:
        steps = jax.random.uniform(jax.random.fold_in(jax.random.fold_in(key, 6), dim), (blocks,), jnp.float32, smallest / len(pieces), top_value / len(pieces))
        level = level * jnp.repeat(jnp.exp(steps), dims[dim] // blocks).reshape((-1,) + (1,) * (len(dims) - 1 - dim))
    return level


def split_up(amount, total, limit, skew):
    portions = [(1 << 20) // math.isqrt(rank ** skew) + 1 for rank in range(2, amount + 1)]
    surplus, holding = total - limit - (amount - 1), [1] * (amount - 1)
    while surplus > 0:
        movable = [i for i in range(amount - 1) if holding[i] < limit]
        pool, left = sum([portions[i] for i in movable]), surplus
        for i in movable:
            addition = min(limit - holding[i], max(1, left * portions[i] // pool), surplus)
            holding[i] = holding[i] + addition
            surplus = surplus - addition
    return np.array([limit] + holding)


def ragged_sizes(own_key, number_of, total, reach, slope):
    if number_of == 2:
        one = jax.random.randint(own_key, (), max(1, total - reach), min(reach, total - 1) + 1)
        return jnp.stack([one, total - one])
    sizes = jnp.asarray(split_up(number_of, total, reach, slope), jnp.int32)
    couples = (number_of - 1) // 2
    source_of, sink = sizes[1:1 + 2 * couples:2], sizes[2:2 + 2 * couples:2]
    room = jnp.minimum(source_of - 1, reach - sink)
    passed = jax.random.randint(jax.random.fold_in(own_key, 1), (couples,), 0, 1 << 20) % (room + 1)
    sizes = sizes.at[1:1 + 2 * couples:2].set(source_of - passed).at[2:2 + 2 * couples:2].set(sink + passed)
    return sizes[jax.random.permutation(jax.random.fold_in(own_key, 2), number_of)]


def gaussian(stream_key, shape, spread, limit, shards=(), kind=jnp.bfloat16):
    entries = spread * jax.random.normal(stream_key, shape, jnp.float32)
    if shards:
        entries = entries * level_of(stream_key, shape, shards, -0.22, 0.18)
    return jnp.clip(entries, -limit, limit).astype(kind)


def setup_inputs(seed: int = 0) -> dict:
    key_list = jax.random.split(jax.random.key(seed), 9)
    return {
        "hidden_in": gaussian(key_list[0], (TOKENS, D), 1.0, 6.0, ((0, 128),)),
        "norm_gain": jnp.clip(1.0 + 0.18 * jax.random.normal(key_list[1], (D,), jnp.float32), 0.1, 1.9),
        "w_qk": draw_w_qk(jax.random.fold_in(key_list[8], 71), 0),
        "w_v": gaussian(key_list[3], (D, KV_HEADS * HEAD_DIM), D ** -0.5, 0.125, ((0, 128),)),
        "w_o": gaussian(key_list[4], (HEADS * HEAD_DIM, D), (HEADS * HEAD_DIM) ** -0.5, 0.125, ((0, 128),)),
        "prompt_pages": ragged_sizes(key_list[5], NREQ, NPAGES, MAXPG, 2).astype(jnp.int32),
        "last_fill": place_ends(jax.random.randint(key_list[6], (NREQ,), 1, PAGE + 1), jax.random.fold_in(key_list[6], 1), 1, PAGE).astype(jnp.int32),
        "page_slots": draw_page_slots(jax.random.fold_in(key_list[8], 71), 0),
    }


THETA = 1000000.0
EPS = 1e-05
NEG = -1e+30

def token_tables(prompt_pages, last_fill):
    ends = (jnp.cumsum(prompt_pages) * PAGE).astype(jnp.int32)
    starts = (ends - prompt_pages * PAGE).astype(jnp.int32)
    lengths = ((prompt_pages - 1) * PAGE + last_fill).astype(jnp.int32)
    return (starts, lengths)

def locate(token_ids, starts, lengths):
    inside = (token_ids[:, None] >= starts[None, :]).astype(jnp.int32)
    request = (lax.optimization_barrier(jnp.sum(inside, axis=1)) - 1).astype(jnp.int32)
    match = jnp.arange(starts.shape[0], dtype=jnp.int32)[None, :] == request[:, None]
    start = lax.optimization_barrier(jnp.sum(jnp.where(match, starts[None, :], 0), axis=1)).astype(jnp.int32)
    length = lax.optimization_barrier(jnp.sum(jnp.where(match, lengths[None, :], 0), axis=1)).astype(jnp.int32)
    position = (token_ids - start).astype(jnp.int32)
    valid = (position < length) & (token_ids >= 0)
    return (request, position, valid)

def pair_mask(query_ids, key_ids, starts, lengths):
    query_req, _, query_valid = locate(query_ids, starts, lengths)
    key_req, _, key_valid = locate(key_ids, starts, lengths)
    allowed = (query_req[:, None] == key_req[None, :]) & (key_ids[None, :] <= query_ids[:, None])
    return (allowed & query_valid[:, None] & key_valid[None, :], query_valid)

def rotate(heads, position):
    half = heads.shape[-1] // 2
    freq = jnp.power(THETA, -2.0 * jnp.arange(half, dtype=jnp.float32) / heads.shape[-1])
    angle = position.astype(jnp.float32)[:, None] * freq[None, :]
    cosine = jnp.concatenate([jnp.cos(angle), jnp.cos(angle)], axis=-1)[:, None, :]
    sine = jnp.concatenate([jnp.sin(angle), jnp.sin(angle)], axis=-1)[:, None, :]
    turned = jnp.concatenate([-heads[..., half:], heads[..., :half]], axis=-1)
    return heads * cosine + turned * sine

def normalize(hidden_in, norm_gain):
    values = hidden_in.astype(jnp.float32)
    scale = lax.rsqrt(lax.optimization_barrier(jnp.mean(values * values, axis=-1, keepdims=True)) + EPS)
    return (values * scale * norm_gain.astype(jnp.float32)[None, :]).astype(jnp.bfloat16)

def split_heads(projected, value_part, position):
    count = projected.shape[0]
    width = HEADS * HEAD_DIM
    queries = rotate(projected[:, :width].reshape(count, HEADS, HEAD_DIM), position)
    queries = queries.astype(jnp.bfloat16).reshape(count, width)
    keys = rotate(projected[:, width:].reshape(count, KV_HEADS, HEAD_DIM), position)
    keys = keys.astype(jnp.bfloat16).reshape(count, KV_HEADS * HEAD_DIM)
    return (queries, keys, value_part.astype(jnp.bfloat16))

def reference(hidden_in, norm_gain, w_qk, w_v, w_o, prompt_pages, last_fill, page_slots):
    starts, lengths = token_tables(prompt_pages, last_fill)
    token_ids = jnp.arange(TOKENS, dtype=jnp.int32)
    _, position, valid = locate(token_ids, starts, lengths)
    normed = normalize(hidden_in, norm_gain)
    projected = jnp.dot(normed, w_qk, preferred_element_type=jnp.float32)
    value_part = jnp.dot(normed, w_v, preferred_element_type=jnp.float32)
    queries, keys, values = split_heads(projected, value_part, position)
    span = REACH * TOK_DEV
    width = KV_HEADS * HEAD_DIM
    front = jnp.zeros((span, width), jnp.bfloat16)
    keys_padded = jnp.concatenate([front, keys], axis=0)
    values_padded = jnp.concatenate([front, values], axis=0)
    group = HEADS // KV_HEADS
    scale = 1.0 / math.sqrt(HEAD_DIM)

    def one_block(index):
        first = (index * TOK_DEV).astype(jnp.int32)
        query_ids = (first + jnp.arange(TOK_DEV, dtype=jnp.int32)).astype(jnp.int32)
        key_ids = (first - span + jnp.arange(span + TOK_DEV, dtype=jnp.int32)).astype(jnp.int32)
        mask, query_valid = pair_mask(query_ids, key_ids, starts, lengths)
        query_rows = lax.dynamic_slice_in_dim(queries, first, TOK_DEV).astype(jnp.float32)
        query_rows = query_rows.reshape(TOK_DEV, KV_HEADS, group, HEAD_DIM)
        key_rows = lax.dynamic_slice_in_dim(keys_padded, first, span + TOK_DEV).astype(jnp.float32)
        key_rows = key_rows.reshape(span + TOK_DEV, KV_HEADS, HEAD_DIM)
        value_rows = lax.dynamic_slice_in_dim(values_padded, first, span + TOK_DEV).astype(jnp.float32)
        value_rows = value_rows.reshape(span + TOK_DEV, KV_HEADS, HEAD_DIM)
        scores = jnp.einsum('qkgd,skd->kgqs', query_rows, key_rows) * scale
        scores = jnp.where(mask[None, None], scores, NEG)
        top = lax.optimization_barrier(jnp.max(scores, axis=-1))
        expo = jnp.where(mask[None, None], jnp.exp(scores - top[..., None]), 0.0)
        total = lax.optimization_barrier(jnp.sum(expo, axis=-1))
        weights = lax.optimization_barrier(expo.astype(jnp.bfloat16)).astype(jnp.float32)
        numer = jnp.einsum('kgqs,skd->kgqd', weights, value_rows)
        safe = jnp.where(query_valid[None, None, :], total, 1.0)
        result = jnp.where(query_valid[None, None, :, None], numer / safe[..., None], 0.0)
        return result.transpose(2, 0, 1, 3).reshape(TOK_DEV, HEADS * HEAD_DIM).astype(jnp.bfloat16)
    attn = lax.map(one_block, jnp.arange(TOKENS // TOK_DEV, dtype=jnp.int32))
    attn = attn.reshape(TOKENS, HEADS * HEAD_DIM)
    attended = jnp.dot(attn, w_o, preferred_element_type=jnp.float32).astype(jnp.bfloat16)
    kept_keys = jnp.where(valid[:, None], keys, jnp.zeros_like(keys)).reshape(NPAGES, PAGE, width)
    kept_values = jnp.where(valid[:, None], values, jnp.zeros_like(values)).reshape(NPAGES, PAGE, width)
    page_ids = jnp.arange(NPAGES, dtype=jnp.int32)
    target = (page_ids // GROUP_PAGES * GROUP_PAGES + page_slots).astype(jnp.int32)
    key_cache = jnp.zeros((NPAGES, PAGE, width), jnp.bfloat16).at[target].set(kept_keys)
    value_cache = jnp.zeros((NPAGES, PAGE, width), jnp.bfloat16).at[target].set(kept_values)
    return (attended, key_cache, value_cache)
```

```python
import functools
import math

import jax
import jax.numpy as jnp
from jax import lax
from jax.experimental import pallas as pl
from jax.experimental.pallas import tpu as pltpu
from jax.sharding import Mesh, PartitionSpec as P

AXES = ("y", "zl", "x", "c", "zh")
SIZES = (4, 2, 4, 2, 2)
QUAD = ("c", "zh")
DEPTH = 2048
TOK = 512
PAGE = 128
QTOK = 4 * TOK
QPAGES = QTOK // PAGE
CHUNK = 256
THETA = 1000000.0
EPS = 1e-05
NEG = -1e30
BF = jnp.bfloat16
F32 = jnp.float32


def swap(block, axis):
    return lax.ppermute(block, axis, [(0, 1), (1, 0)])


def shift(block, axis, distance):
    return lax.ppermute(block, axis, [(i, (i + distance) % 4) for i in range(4)])


def to_role(block, flip):
    return lax.ppermute(block, QUAD, [(i, i ^ flip) for i in range(4)])


def place(total, piece, index, dim):
    starts = [jnp.int32(0)] * total.ndim
    starts[dim] = index
    return lax.dynamic_update_slice(total, jnp.expand_dims(piece, dim), starts)


def pair_gather(block, axis, dim):
    other = swap(block, axis)
    first = lax.axis_index(axis) == 0
    return jnp.where(
        first, jnp.stack([block, other], dim), jnp.stack([other, block], dim)
    )


def ring_gather(block, axis, dim, relay, row_dim):
    me = lax.axis_index(axis)
    left = shift(block, axis, 1)
    right = shift(block, axis, -1)
    if relay:
        half = block.shape[row_dim] // 2
        near = lax.slice_in_dim(left, 0, half, axis=row_dim)
        far = lax.slice_in_dim(right, half, 2 * half, axis=row_dim)
        opposite = jnp.concatenate(
            [shift(near, axis, 1), shift(far, axis, -1)], axis=row_dim
        )
    else:
        opposite = shift(block, axis, 2)
    shape = block.shape[:dim] + (4,) + block.shape[dim:]
    total = jnp.zeros(shape, block.dtype)
    total = place(total, block, me, dim)
    total = place(total, left, (me + 3) % 4, dim)
    total = place(total, right, (me + 1) % 4, dim)
    return place(total, opposite, (me + 2) % 4, dim)


def normalize(hidden_in, norm_gain):
    values = hidden_in.astype(F32)
    scale = lax.rsqrt(jnp.mean(values * values, axis=-1, keepdims=True) + EPS)
    return (values * scale * norm_gain[None, :]).astype(BF)


def page_tables(prompt_pages, last_fill, first_page):
    count = prompt_pages.shape[0]
    order = jnp.arange(count, dtype=jnp.int32)
    ends = jnp.sum(
        jnp.where(order[None, :] <= order[:, None], prompt_pages[None, :], 0), axis=1
    )
    pages = first_page + jnp.arange(QPAGES, dtype=jnp.int32)
    before = ends[None, :] <= pages[:, None]
    start = jnp.max(jnp.where(before, ends[None, :], 0), axis=1)
    closing = ends[None, :] == pages[:, None] + 1
    short = jnp.sum(jnp.where(closing, PAGE - last_fill[None, :], 0), axis=1)
    return pages - start, PAGE - short


def rotation_tables(offset):
    row = jnp.arange(PAGE, dtype=jnp.int32)
    position = (offset[:, None] * PAGE + row[None, :]).reshape(QTOK)
    half = 64
    freq = jnp.power(THETA, -2.0 * jnp.arange(half, dtype=F32) / 128)
    angle = position.astype(F32)[:, None] * freq[None, :]
    cosine, sine = jnp.cos(angle), jnp.sin(angle)
    return (
        jnp.concatenate([cosine, cosine], axis=-1),
        jnp.concatenate([-sine, sine], axis=-1),
    )


def project_kernel(meta, x_ref, wq_ref, wkv_ref, cos_ref, sin_ref, q_ref, kv_ref):
    x = x_ref[...]
    cosine = cos_ref[...]
    sine = sin_ref[...]

    def turned(block):
        return (block * cosine + pltpu.roll(block, 64, 1) * sine).astype(BF)

    queries = jnp.dot(x, wq_ref[...], preferred_element_type=F32)
    for head in range(4):
        lanes = slice(128 * head, 128 * head + 128)
        q_ref[:, lanes] = turned(queries[:, lanes])
    both = jnp.dot(x, wkv_ref[...], preferred_element_type=F32)
    for head in range(2):
        lanes = slice(128 * head, 128 * head + 128)
        kv_ref[:, lanes] = turned(both[:, lanes])
    kv_ref[:, 256:] = both[:, 256:].astype(BF)


def project(meta, x, w_q, w_kv, cosine, sine, flip):
    tile = 256
    steps = TOK // tile

    def table(i, meta_ref):
        return (jnp.bitwise_xor(meta_ref[0], flip) * steps + i, 0)

    return pl.pallas_call(
        project_kernel,
        grid_spec=pltpu.PrefetchScalarGridSpec(
            num_scalar_prefetch=1,
            grid=(steps,),
            in_specs=[
                pl.BlockSpec((tile, DEPTH), lambda i, m: (i, 0)),
                pl.BlockSpec((DEPTH, 512), lambda i, m: (0, 0)),
                pl.BlockSpec((DEPTH, 512), lambda i, m: (0, 0)),
                pl.BlockSpec((tile, 128), table),
                pl.BlockSpec((tile, 128), table),
            ],
            out_specs=[
                pl.BlockSpec((tile, 512), lambda i, m: (i, 0)),
                pl.BlockSpec((tile, 512), lambda i, m: (i, 0)),
            ],
        ),
        out_shape=[jax.ShapeDtypeStruct((TOK, 512), BF)] * 2,
        compiler_params=pltpu.CompilerParams(vmem_limit_bytes=40 << 20),
        cost_estimate=pl.CostEstimate(
            flops=2 * TOK * DEPTH * 1024, transcendentals=0, bytes_accessed=8 << 20
        ),
        name=f"project_{flip}",
    )(meta, x, w_q, w_kv, cosine, sine)


def attend_kernel(flips, meta, *refs):
    q_refs, own_refs, halo_refs = refs[:2], refs[2:6], refs[6:10]
    out_refs, kv, sems = refs[10:12], refs[12], refs[13]
    role = meta[0]
    copies = []
    for p in range(4):
        block = jnp.bitwise_xor(role, p)
        for at, source in ((0, halo_refs[p]), (4, own_refs[p])):
            rows = pl.ds(pl.multiple_of((block + at) * TOK, TOK), TOK)
            copies.append(
                pltpu.make_async_copy(source, kv.at[rows, :], sems.at[p + at])
            )
    for copy in copies:
        copy.start()
    for copy in copies:
        copy.wait()
    factor = (1.0 / math.sqrt(128)) * math.log2(math.e)
    row = lax.broadcasted_iota(jnp.int32, (256, CHUNK), 0) % PAGE
    lane = lax.broadcasted_iota(jnp.int32, (256, CHUNK), 1)
    gap = lane - row
    tall = lax.broadcasted_iota(jnp.int32, (PAGE, 128), 0)
    for q_ref, out_ref, flip in zip(q_refs, out_refs, flips):
        first = jnp.bitwise_xor(role, flip) * 4

        def one_page(page, carry, q_ref=q_ref, out_ref=out_ref, first=first):
            rows = pl.ds(pl.multiple_of(page * PAGE, PAGE), PAGE)
            at = QTOK + (first + page) * PAGE
            low = at - meta[1 + first + page] * PAGE
            live = meta[17 + first + page]
            tops, stack = [], []
            for h in range(2):
                stack.append(
                    jnp.concatenate(
                        [
                            q_ref[rows, 256 * h : 256 * h + 128],
                            q_ref[rows, 256 * h + 128 : 256 * h + 256],
                        ],
                        axis=0,
                    )
                )

            def one_chunk(chunk, state):
                base = pl.multiple_of(chunk * CHUNK, CHUNK)
                keep = (lane >= low - base) & (gap <= at - base)
                result = []
                for h in range(2):
                    top, total, acc = state[h]
                    keys = kv[pl.ds(base, CHUNK), 128 * h : 128 * h + 128]
                    vals = kv[pl.ds(base, CHUNK), 256 + 128 * h : 384 + 128 * h]
                    scores = lax.dot_general(
                        stack[h],
                        keys,
                        (((1,), (1,)), ((), ())),
                        preferred_element_type=F32,
                    )
                    scores = jnp.where(keep, scores, NEG)
                    higher = jnp.maximum(top, jnp.max(scores, axis=1, keepdims=True))
                    fade = jnp.exp2((top - higher) * factor)
                    expo = jnp.exp2((scores - higher) * factor)
                    total = total * fade + jnp.sum(expo, axis=1, keepdims=True)
                    acc = acc * fade + jnp.dot(
                        expo.astype(BF), vals, preferred_element_type=F32
                    )
                    result.append((higher, total, acc))
                return tuple(result)

            empty = (
                jnp.full((256, 1), NEG, F32),
                jnp.zeros((256, 1), F32),
                jnp.zeros((256, 128), F32),
            )
            state = lax.fori_loop(
                low // CHUNK, at // CHUNK + 1, one_chunk, (empty, empty)
            )
            for h in range(2):
                _, total, acc = state[h]
                value = acc / total
                for g in range(2):
                    part = value[128 * g : 128 * g + 128]
                    part = jnp.where(tall < live, part, 0.0)
                    at_lane = 256 * h + 128 * g
                    out_ref[rows, at_lane : at_lane + 128] = part.astype(BF)
            return carry

        lax.fori_loop(0, 4, one_page, 0)


def attend(meta, queries, own, halo, flips):
    whole = pl.BlockSpec((TOK, 512), lambda i, m: (0, 0))
    hbm = pl.BlockSpec(memory_space=pl.ANY)
    return pl.pallas_call(
        functools.partial(attend_kernel, flips),
        grid_spec=pltpu.PrefetchScalarGridSpec(
            num_scalar_prefetch=1,
            grid=(1,),
            in_specs=[whole] * 2 + [hbm] * 8,
            out_specs=[whole] * 2,
            scratch_shapes=[
                pltpu.VMEM((2 * QTOK, 512), BF),
                pltpu.SemaphoreType.DMA((8,)),
            ],
        ),
        out_shape=[jax.ShapeDtypeStruct((TOK, 512), BF)] * 2,
        compiler_params=pltpu.CompilerParams(vmem_limit_bytes=40 << 20),
        cost_estimate=pl.CostEstimate(
            flops=4 << 30, transcendentals=4 << 20, bytes_accessed=6 << 20
        ),
        name=f"attend_{flips[0]}",
    )(meta, *queries, *own, *halo)


def pack_kernel(meta, *refs):
    own_refs, out_refs, kv, sems = refs[:4], refs[4:8], refs[8], refs[9]
    role = meta[0]
    copies = []
    for p in range(4):
        rows = pl.ds(pl.multiple_of(jnp.bitwise_xor(role, p) * TOK, TOK), TOK)
        copies.append(pltpu.make_async_copy(own_refs[p], kv.at[rows, :], sems.at[p]))
    for copy in copies:
        copy.start()
    for copy in copies:
        copy.wait()
    tall = lax.broadcasted_iota(jnp.int32, (PAGE, 512), 0)
    for p in range(4):
        target = jnp.bitwise_xor(role, p)
        for slot in range(4):
            page = meta[33 + target * 4 + slot]
            live = meta[17 + page]
            rows = pl.ds(pl.multiple_of(page * PAGE, PAGE), PAGE)
            block = jnp.where(tall < live, kv[rows, :].astype(F32), 0.0)
            out_refs[p][PAGE * slot : PAGE * slot + PAGE, :] = block.astype(BF)


def pack(meta, own):
    whole = pl.BlockSpec((TOK, 512), lambda i, m: (0, 0))
    hbm = pl.BlockSpec(memory_space=pl.ANY)
    return pl.pallas_call(
        pack_kernel,
        grid_spec=pltpu.PrefetchScalarGridSpec(
            num_scalar_prefetch=1,
            grid=(1,),
            in_specs=[hbm] * 4,
            out_specs=[whole] * 4,
            scratch_shapes=[
                pltpu.VMEM((QTOK, 512), BF),
                pltpu.SemaphoreType.DMA((4,)),
            ],
        ),
        out_shape=[jax.ShapeDtypeStruct((TOK, 512), BF)] * 4,
        compiler_params=pltpu.CompilerParams(vmem_limit_bytes=30 << 20),
        name="pack_pages",
    )(meta, *own)


def unpack_kernel(meta, *refs):
    in_refs, key_ref, value_ref = refs[:4], refs[4], refs[5]
    step = pl.program_id(0)
    for p in range(4):

        @pl.when(step == p)
        def _(p=p):
            key_ref[...] = in_refs[p][:, :256]
            value_ref[...] = in_refs[p][:, 256:]


def unpack(meta, received):
    whole = pl.BlockSpec((TOK, 512), lambda i, m: (0, 0))
    column = pl.BlockSpec((TOK, 256), lambda i, m: (0, jnp.bitwise_xor(m[0], i)))
    return pl.pallas_call(
        unpack_kernel,
        grid_spec=pltpu.PrefetchScalarGridSpec(
            num_scalar_prefetch=1,
            grid=(4,),
            in_specs=[whole] * 4,
            out_specs=[column] * 2,
        ),
        out_shape=[jax.ShapeDtypeStruct((TOK, 1024), BF)] * 2,
        compiler_params=pltpu.CompilerParams(vmem_limit_bytes=30 << 20),
        name="unpack_pages",
    )(meta, *received)


def output_kernel(meta, *refs):
    in_refs, weight_refs, out_ref = refs[:4], refs[4:6], refs[6]
    step = pl.program_id(0)
    for half in range(2):

        @pl.when(step == half)
        def _(half=half):
            total = jnp.zeros((TOK, 1024), F32)
            for p in range(4):
                start = pl.multiple_of(jnp.bitwise_xor(meta[0], p) * 512, 512)
                total += jnp.dot(
                    in_refs[p][...],
                    weight_refs[half][pl.ds(start, 512), :],
                    preferred_element_type=F32,
                )
            out_ref[...] = total.astype(BF)


def output(meta, received, own_half, other_half):
    whole = pl.BlockSpec((TOK, 512), lambda i, m: (0, 0))
    weight = pl.BlockSpec((DEPTH, 1024), lambda i, m: (0, 0))
    return pl.pallas_call(
        output_kernel,
        grid_spec=pltpu.PrefetchScalarGridSpec(
            num_scalar_prefetch=1,
            grid=(2,),
            in_specs=[whole] * 4 + [weight] * 2,
            out_specs=pl.BlockSpec(
                (TOK, 1024), lambda i, m: (0, jnp.bitwise_xor(m[0] // 2, i))
            ),
        ),
        out_shape=jax.ShapeDtypeStruct((TOK, DEPTH), BF),
        compiler_params=pltpu.CompilerParams(vmem_limit_bytes=48 << 20),
        name="output_rows",
    )(meta, *received, own_half, other_half)


def page_sources(page_slots, core):
    other = swap(page_slots, "c")
    first = jnp.where(core == 0, page_slots, other)
    second = jnp.where(core == 0, other, page_slots)
    slots = jnp.stack([first, second])
    wanted = jnp.arange(8, dtype=jnp.int32)
    hit = slots[:, None, :] == wanted[None, :, None]
    found = jnp.sum(jnp.where(hit, wanted[None, None, :], 0), axis=2)
    return (found + jnp.array([[0], [8]], jnp.int32)).reshape(16)


def previous_quad(block):
    names = ("y", "zl", "x", "c", "zh")
    route = [(i, i + 4) for i in range(124)]
    return lax.ppermute(block, names, route)


def gather_qkv(w_qk, w_v):
    rows = w_qk.shape[0]
    pieces = jnp.concatenate(
        [
            w_qk[:, :2048].reshape(rows, 4, 512),
            w_qk[:, 2048:].reshape(rows, 4, 256),
            w_v.reshape(rows, 4, 256),
        ],
        axis=2,
    ).transpose(1, 0, 2)
    mine = lax.all_to_all(pieces, QUAD, split_axis=0, concat_axis=0, tiled=True)
    mine = mine.reshape(4 * rows, 1024)
    level = pair_gather(mine, "zl", 0)
    query = ring_gather(level[:, :, :512], "x", 1, False, 1)
    both = ring_gather(level[:, :, 512:], "y", 0, False, 1)
    query = ring_gather(query, "y", 0, True, 2)
    both = ring_gather(both, "x", 2, True, 2)
    return query.reshape(DEPTH, 512), both.reshape(DEPTH, 512)


def gather_output(w_o, core):
    halves = w_o.reshape(16, 2, 1024)
    kept = lax.dynamic_index_in_dim(halves, core, 1, keepdims=False)
    sent = lax.dynamic_index_in_dim(halves, 1 - core, 1, keepdims=False)
    got = swap(sent, "c")
    level = jnp.where(core == 0, jnp.stack([kept, got]), jnp.stack([got, kept]))
    level = pair_gather(level, "zh", 1)
    level = pair_gather(level.reshape(64, 1024), "zl", 0)
    level = ring_gather(level, "x", 1, False, 1)
    level = ring_gather(level, "y", 0, True, 2)
    half = level.reshape(DEPTH, 1024)
    return half, swap(half, "c")


def shards(hidden_in, norm_gain, w_qk, w_v, w_o, prompt_pages, last_fill, page_slots):
    core = lax.axis_index("c")
    role = core * 2 + lax.axis_index("zh")
    quad = (lax.axis_index("y") * 2 + lax.axis_index("zl")) * 4 + lax.axis_index("x")
    offset, live = page_tables(prompt_pages, last_fill, quad * QPAGES)
    sources = page_sources(page_slots, core)
    meta = jnp.concatenate([role[None], offset, live, sources]).astype(jnp.int32)
    cosine, sine = rotation_tables(offset)

    normed = [normalize(hidden_in, norm_gain)]
    w_q, w_kv = gather_qkv(w_qk, w_v)
    normed.append(swap(normed[0], "zh"))
    normed.append(swap(normed[0], "c"))
    normed.append(swap(normed[1], "c"))

    queries, own, halo = [None] * 4, [None] * 4, [None] * 4
    for flip in (0, 2, 1, 3):
        queries[flip], own[flip] = project(
            meta, normed[flip], w_q, w_kv, cosine, sine, flip
        )
        halo[flip] = previous_quad(own[flip])
    packed = pack(meta, own)
    far = attend(meta, (queries[1], queries[3]), own, halo, (1, 3))
    near = attend(meta, (queries[0], queries[2]), own, halo, (0, 2))
    received = [
        near[0],
        to_role(far[0], 1),
        to_role(near[1], 2),
        to_role(far[1], 3),
    ]
    own_half, other_half = gather_output(w_o, core)
    attended = output(meta, received, own_half, other_half)
    pages = [packed[0]] + [to_role(packed[flip], flip) for flip in (1, 2, 3)]
    key_cache, value_cache = unpack(meta, pages)
    return (
        attended,
        key_cache.reshape(4, PAGE, 1024),
        value_cache.reshape(4, PAGE, 1024),
    )


def solution(mesh):
    fine = Mesh(mesh.devices.reshape(SIZES), AXES)
    rows = P(AXES, None)
    in_specs = (rows, P(), rows, rows, rows, P(), P(), P(("y", "zl", "x", "c")))
    out_specs = (rows, P(AXES, None, None), P(AXES, None, None))
    return jax.shard_map(
        shards, mesh=fine, in_specs=in_specs, out_specs=out_specs, check_vma=False
    )
```

```python
import functools
import math

import jax
import jax.numpy as jnp
from jax import lax
from jax.experimental import pallas as pl
from jax.experimental.pallas import tpu as pltpu
from jax.sharding import Mesh, PartitionSpec as P

AXES = ("y", "zl", "x", "c", "zh")
SIZES = (4, 2, 4, 2, 2)
QUAD = ("c", "zh")
DEPTH = 2048
TOK = 512
PAGE = 128
QTOK = 4 * TOK
QPAGES = QTOK // PAGE
CHUNK = 256
THETA = 1000000.0
EPS = 1e-05
NEG = -1e30
BF = jnp.bfloat16
F32 = jnp.float32


def swap(block, axis):
    return lax.ppermute(block, axis, [(0, 1), (1, 0)])


def shift(block, axis, distance):
    return lax.ppermute(block, axis, [(i, (i + distance) % 4) for i in range(4)])


def to_role(block, flip):
    return lax.ppermute(block, QUAD, [(i, i ^ flip) for i in range(4)])


def pair_gather(block, axis):
    other = swap(block, axis)
    first = lax.axis_index(axis) == 0
    return jnp.where(first, jnp.stack([block, other]), jnp.stack([other, block]))


def ring_pieces(block, axis):
    return [block] + [shift(block, axis, distance) for distance in (1, 2, 3)]


def after(block, *others):
    return lax.optimization_barrier((block, *others))[0]


def normalize(hidden_in, norm_gain):
    values = hidden_in.astype(F32)
    scale = lax.rsqrt(jnp.mean(values * values, axis=-1, keepdims=True) + EPS)
    return (values * scale * norm_gain[None, :]).astype(BF)


def page_tables(prompt_pages, last_fill, first_page):
    count = prompt_pages.shape[0]
    order = jnp.arange(count, dtype=jnp.int32)
    ends = jnp.sum(
        jnp.where(order[None, :] <= order[:, None], prompt_pages[None, :], 0), axis=1
    )
    pages = first_page + jnp.arange(QPAGES, dtype=jnp.int32)
    before = ends[None, :] <= pages[:, None]
    start = jnp.max(jnp.where(before, ends[None, :], 0), axis=1)
    closing = ends[None, :] == pages[:, None] + 1
    short = jnp.sum(jnp.where(closing, PAGE - last_fill[None, :], 0), axis=1)
    return pages - start, PAGE - short


def rotation_tables(offset):
    row = jnp.arange(PAGE, dtype=jnp.int32)
    position = (offset[:, None] * PAGE + row[None, :]).reshape(QTOK)
    half = 64
    freq = jnp.power(THETA, -2.0 * jnp.arange(half, dtype=F32) / 128)
    angle = position.astype(F32)[:, None] * freq[None, :]
    cosine, sine = jnp.cos(angle), jnp.sin(angle)
    return (
        jnp.concatenate([cosine, cosine], axis=-1),
        jnp.concatenate([-sine, sine], axis=-1),
    )


def fill_weight(here, pieces, weight, sems, along_y, first_sem=0):
    y, x = here
    copies = []
    for i in range(4):
        for k in range(4):
            dy, dx = (i, k) if along_y else (k, i)
            target = weight.at[lax.rem(y + 4 - dy, 4), :, lax.rem(x + 4 - dx, 4)]
            sem = sems.at[first_sem + 4 * i + k]
            copies.append(pltpu.make_async_copy(pieces[i].at[k], target, sem))
    return copies


def project_kernel(meta, *refs):
    x_refs, q_parts, kv_parts, tables = refs[:2], refs[2:6], refs[6:10], refs[10:12]
    q_ref, kvt_ref, v_ref, w_q, w_kv, sems = refs[12:]
    step = pl.program_id(0)

    @pl.when(step == 0)
    def _():
        here = (meta[49], meta[50])
        copies = fill_weight(here, q_parts, w_q, sems, True)
        copies += fill_weight(here, kv_parts, w_kv, sems, False, 16)
        for copy in copies:
            copy.start()
        for copy in copies:
            copy.wait()

    cosine = tables[0][...]
    sine = tables[1][...]

    def turned(block):
        return (block * cosine + pltpu.roll(block, 64, 1) * sine).astype(BF)

    def body(x):
        queries = jnp.dot(
            x, w_q[...].reshape(DEPTH, 512), preferred_element_type=F32
        )
        for head in range(4):
            lanes = slice(128 * head, 128 * head + 128)
            q_ref[:, lanes] = turned(queries[:, lanes])
        both = jnp.dot(
            x, w_kv[...].reshape(DEPTH, 512), preferred_element_type=F32
        )
        for head in range(2):
            kvt_ref[head] = turned(both[:, 128 * head : 128 * head + 128])
            value = both[:, 256 + 128 * head : 384 + 128 * head]
            v_ref[head] = value.astype(BF)
            for page in range(x.shape[0] // PAGE):
                rows = slice(PAGE * page, PAGE * page + PAGE)
                kvt_ref[2 + head, rows, :] = jnp.transpose(value[rows]).astype(BF)

    @pl.when(step < 2)
    def _():
        body(x_refs[0][...])

    @pl.when(step >= 2)
    def _():
        body(x_refs[1][...])


def project(meta, first, second, q_parts, kv_parts, cosine, sine, pair):
    tile = 256

    def table(i, m):
        return (jnp.bitwise_xor(m[0], 2 * (i // 2) + pair) * 2 + i % 2, 0)

    hbm = pl.BlockSpec(memory_space=pl.ANY)
    return pl.pallas_call(
        project_kernel,
        grid_spec=pltpu.PrefetchScalarGridSpec(
            num_scalar_prefetch=1,
            grid=(4,),
            in_specs=[
                pl.BlockSpec((tile, DEPTH), lambda i, m: (jnp.minimum(i, 1), 0)),
                pl.BlockSpec((tile, DEPTH), lambda i, m: (jnp.maximum(i - 2, 0), 0)),
            ]
            + [hbm] * 8
            + [pl.BlockSpec((tile, 128), table)] * 2,
            out_specs=[
                pl.BlockSpec((tile, 512), lambda i, m: (i, 0)),
                pl.BlockSpec((4, tile, 128), lambda i, m: (0, i, 0)),
                pl.BlockSpec((2, tile, 128), lambda i, m: (0, i, 0)),
            ],
            scratch_shapes=[
                pltpu.VMEM((4, 2, 4, 64, 512), BF),
                pltpu.VMEM((4, 2, 4, 64, 512), BF),
                pltpu.SemaphoreType.DMA((32,)),
            ],
        ),
        out_shape=[
            jax.ShapeDtypeStruct((2 * TOK, 512), BF),
            jax.ShapeDtypeStruct((4, 2 * TOK, 128), BF),
            jax.ShapeDtypeStruct((2, 2 * TOK, 128), BF),
        ],
        compiler_params=pltpu.CompilerParams(vmem_limit_bytes=40 << 20),
        cost_estimate=pl.CostEstimate(
            flops=4 * TOK * DEPTH * 1024, transcendentals=0, bytes_accessed=12 << 20
        ),
        name=f"project_{pair}",
    )(meta, first, second, *q_parts, *kv_parts, cosine, sine)


def attend_kernel(pair, meta, *refs):
    q_ref, own, halo, out_ref, kvt, saved, bias, sems = (
        refs[0], refs[1:3], refs[3:5], *refs[5:]
    )
    role = meta[0]
    copies = []
    for p in range(4):
        block = jnp.bitwise_xor(role, 2 * (p % 2) + p // 2)
        source = pl.ds((p % 2) * TOK, TOK)
        for at, side in ((0, halo), (4, own)):
            rows = pl.ds(pl.multiple_of((block + at) * TOK, TOK), TOK)
            copies.append(
                pltpu.make_async_copy(
                    side[p // 2].at[:, source, :], kvt.at[:, rows, :], sems.at[p + at]
                )
            )
    for copy in copies:
        copy.start()
    kvt[:, pl.ds(2 * QTOK, CHUNK), :] = jnp.zeros((4, CHUNK, 128), BF)
    gap = lax.broadcasted_iota(jnp.int32, (CHUNK, 256), 0) - (
        lax.broadcasted_iota(jnp.int32, (CHUNK, 256), 1) % PAGE
    )
    for i in range(2):
        bias[i] = jnp.where(gap <= i * PAGE, 0.0, NEG)
    for copy in copies:
        copy.wait()
    factor = (1.0 / math.sqrt(128)) * math.log2(math.e)
    tall = lax.broadcasted_iota(jnp.int32, (PAGE, 128), 0)

    def one_page(index, carry):
        rows = pl.ds(pl.multiple_of(index * PAGE, PAGE), PAGE)
        page = jnp.bitwise_xor(role, 2 * (index // 4) + pair) * 4 + index % 4
        offset = meta[1 + page]
        live = meta[17 + page]
        low = QPAGES + page - offset
        full = offset // 2
        stack = [
            jnp.concatenate(
                [
                    q_ref[rows, 256 * h : 256 * h + 128],
                    q_ref[rows, 256 * h + 128 : 256 * h + 256],
                ],
                axis=0,
            )
            for h in range(2)
        ]

        def scan(chunk, tops, count, masked):
            base = pl.multiple_of((low + 2 * chunk) * PAGE, PAGE)
            result = []
            for h in range(2):
                scores = lax.dot_general(
                    kvt[h, pl.ds(base, count * CHUNK), :],
                    stack[h],
                    (((1,), (1,)), ((), ())),
                    preferred_element_type=F32,
                )
                if masked:
                    scores = scores + bias[offset % 2]
                for i in range(count):
                    saved[h, chunk + i] = scores[CHUNK * i : CHUNK * i + CHUNK]
                peak = jnp.max(scores.reshape(count * CHUNK // 8, 8, 256), axis=0)
                result.append(jnp.maximum(tops[h], peak))
            return tuple(result)

        tops = (jnp.full((8, 256), NEG, F32),) * 2
        tops = lax.fori_loop(
            0, full // 2, lambda i, t: scan(2 * i, t, 2, False), tops
        )
        tops = lax.fori_loop(
            full // 2 * 2, full, lambda i, t: scan(i, t, 1, False), tops
        )
        tops = scan(full, tops, 1, True)
        tops = [jnp.max(top, axis=0, keepdims=True) for top in tops]

        def fold(chunk, state, count):
            result = []
            for h in range(2):
                total, acc = state[h]
                parts, weights = [], []
                for i in range(count):
                    expo = jnp.exp2((saved[h, chunk + i] - tops[h]) * factor)
                    total = total + jnp.sum(expo.reshape(CHUNK // 8, 8, 256), axis=0)
                    weights.append(expo.astype(BF))
                for i in range(2 * count):
                    at = pl.multiple_of((low + 2 * chunk + i) * PAGE, PAGE)
                    parts.append(kvt[2 + h, pl.ds(at, PAGE), :])
                acc = acc + jnp.dot(
                    jnp.concatenate(parts, axis=1),
                    jnp.concatenate(weights, axis=0),
                    preferred_element_type=F32,
                )
                result.append((total, acc))
            return tuple(result)

        state = ((jnp.zeros((8, 256), F32), jnp.zeros((128, 256), F32)),) * 2
        count = full + 1
        state = lax.fori_loop(0, count // 2, lambda i, s: fold(2 * i, s, 2), state)
        state = lax.fori_loop(
            count // 2 * 2, count, lambda i, s: fold(i, s, 1), state
        )
        for h in range(2):
            total, acc = state[h]
            value = acc / jnp.sum(total, axis=0, keepdims=True)
            value = jnp.transpose(value)
            for g in range(2):
                part = value[128 * g : 128 * g + 128]
                part = jnp.where(tall < live, part, 0.0)
                at_lane = 256 * h + 128 * g
                out_ref[rows, at_lane : at_lane + 128] = part.astype(BF)
        return carry

    lax.fori_loop(0, 8, one_page, 0)


def attend(meta, queries, own, halo, pair):
    whole = pl.BlockSpec((2 * TOK, 512), lambda i, m: (0, 0))
    hbm = pl.BlockSpec(memory_space=pl.ANY)
    return pl.pallas_call(
        functools.partial(attend_kernel, pair),
        grid_spec=pltpu.PrefetchScalarGridSpec(
            num_scalar_prefetch=1,
            grid=(1,),
            in_specs=[whole] + [hbm] * 4,
            out_specs=whole,
            scratch_shapes=[
                pltpu.VMEM((4, 2 * QTOK + CHUNK, 128), BF),
                pltpu.VMEM((2, 9, CHUNK, 256), F32),
                pltpu.VMEM((2, CHUNK, 256), F32),
                pltpu.SemaphoreType.DMA((8,)),
            ],
        ),
        out_shape=jax.ShapeDtypeStruct((2 * TOK, 512), BF),
        compiler_params=pltpu.CompilerParams(vmem_limit_bytes=40 << 20),
        cost_estimate=pl.CostEstimate(
            flops=4 << 30, transcendentals=4 << 20, bytes_accessed=6 << 20
        ),
        name=f"attend_{pair}",
    )(meta, queries, *own, *halo)


def pack_kernel(meta, *refs):
    keys, values, out_refs, kv, sems = refs[:2], refs[2:4], refs[4:8], refs[8], refs[9]
    role = meta[0]
    copies = []
    for p in range(4):
        block = jnp.bitwise_xor(role, 2 * (p % 2) + p // 2)
        rows = pl.ds(pl.multiple_of(block * TOK, TOK), TOK)
        source = pl.ds((p % 2) * TOK, TOK)
        for at, side in ((0, keys), (2, values)):
            copies.append(
                pltpu.make_async_copy(
                    side[p // 2].at[pl.ds(0, 2), source, :],
                    kv.at[pl.ds(at, 2), rows, :],
                    sems.at[p + 2 * at],
                )
            )
    for copy in copies:
        copy.start()
    for copy in copies:
        copy.wait()
    tall = lax.broadcasted_iota(jnp.int32, (PAGE, 128), 0)
    for p in range(4):
        target = jnp.bitwise_xor(role, p)
        for slot in range(4):
            page = meta[33 + target * 4 + slot]
            live = meta[17 + page]
            rows = pl.ds(pl.multiple_of(page * PAGE, PAGE), PAGE)
            for part in range(4):
                block = jnp.where(tall < live, kv[part, rows, :].astype(F32), 0.0)
                lanes = slice(128 * part, 128 * part + 128)
                out_refs[p][PAGE * slot : PAGE * slot + PAGE, lanes] = block.astype(BF)


def pack(meta, keys, values):
    whole = pl.BlockSpec((TOK, 512), lambda i, m: (0, 0))
    hbm = pl.BlockSpec(memory_space=pl.ANY)
    return pl.pallas_call(
        pack_kernel,
        grid_spec=pltpu.PrefetchScalarGridSpec(
            num_scalar_prefetch=1,
            grid=(1,),
            in_specs=[hbm] * 4,
            out_specs=[whole] * 4,
            scratch_shapes=[
                pltpu.VMEM((4, QTOK, 128), BF),
                pltpu.SemaphoreType.DMA((8,)),
            ],
        ),
        out_shape=[jax.ShapeDtypeStruct((TOK, 512), BF)] * 4,
        compiler_params=pltpu.CompilerParams(vmem_limit_bytes=30 << 20),
        name="pack_pages",
    )(meta, *keys, *values)


def unpack_kernel(meta, *refs):
    in_refs, key_ref, value_ref = refs[:4], refs[4], refs[5]
    step = pl.program_id(0)
    for p in range(4):

        @pl.when(step == p)
        def _(p=p):
            key_ref[...] = in_refs[p][:, :256]
            value_ref[...] = in_refs[p][:, 256:]


def unpack(meta, received):
    whole = pl.BlockSpec((TOK, 512), lambda i, m: (0, 0))
    column = pl.BlockSpec((TOK, 256), lambda i, m: (0, jnp.bitwise_xor(m[0], i)))
    return pl.pallas_call(
        unpack_kernel,
        grid_spec=pltpu.PrefetchScalarGridSpec(
            num_scalar_prefetch=1,
            grid=(4,),
            in_specs=[whole] * 4,
            out_specs=[column] * 2,
        ),
        out_shape=[jax.ShapeDtypeStruct((TOK, 1024), BF)] * 2,
        compiler_params=pltpu.CompilerParams(vmem_limit_bytes=30 << 20),
        name="unpack_pages",
    )(meta, *received)


def output_kernel(meta, *refs):
    in_refs, parts, out_ref, weight, sems = refs[:4], refs[4:6], *refs[6:]
    step = pl.program_id(0)
    here = (meta[49], meta[50])
    copies = [
        fill_weight(here, [parts[h].at[i] for i in range(4)], weight.at[h], sems, True, 16 * h)
        for h in range(2)
    ]

    @pl.when(step == 0)
    def _():
        for copy in copies[0] + copies[1]:
            copy.start()

    for half in range(2):

        @pl.when(step == half)
        def _(half=half):
            for copy in copies[half]:
                copy.wait()
            rows = weight.at[half]
            total = jnp.zeros((TOK, 1024), F32)
            for p in range(4):
                block = jnp.bitwise_xor(meta[0], p)
                total += jnp.dot(
                    in_refs[p][...],
                    rows[block].reshape(512, 1024),
                    preferred_element_type=F32,
                )
            out_ref[...] = total.astype(BF)


def output(meta, received, own_half, other_half):
    whole = pl.BlockSpec((TOK, 512), lambda i, m: (0, 0))
    hbm = pl.BlockSpec(memory_space=pl.ANY)
    return pl.pallas_call(
        output_kernel,
        grid_spec=pltpu.PrefetchScalarGridSpec(
            num_scalar_prefetch=1,
            grid=(2,),
            in_specs=[whole] * 4 + [hbm] * 2,
            out_specs=pl.BlockSpec(
                (TOK, 1024), lambda i, m: (0, jnp.bitwise_xor(m[0] // 2, i))
            ),
            scratch_shapes=[
                pltpu.VMEM((2, 4, 2, 4, 64, 1024), BF),
                pltpu.SemaphoreType.DMA((32,)),
            ],
        ),
        out_shape=jax.ShapeDtypeStruct((TOK, DEPTH), BF),
        compiler_params=pltpu.CompilerParams(vmem_limit_bytes=48 << 20),
        name="output_rows",
    )(meta, *received, own_half, other_half)


def page_sources(page_slots, core):
    other = swap(page_slots, "c")
    first = jnp.where(core == 0, page_slots, other)
    second = jnp.where(core == 0, other, page_slots)
    slots = jnp.stack([first, second])
    wanted = jnp.arange(8, dtype=jnp.int32)
    hit = slots[:, None, :] == wanted[None, :, None]
    found = jnp.sum(jnp.where(hit, wanted[None, None, :], 0), axis=2)
    return (found + jnp.array([[0], [8]], jnp.int32)).reshape(16)


def previous_quad(block):
    names = ("y", "zl", "x", "c", "zh")
    route = [(i, i + 4) for i in range(124)]
    return lax.ppermute(block, names, route)


def role_slices(w_qk, w_v, w_o):
    rows = w_qk.shape[0]
    halves = w_o.reshape(rows, 2, 1024)
    return jnp.concatenate(
        [
            w_qk[:, :2048].reshape(rows, 4, 512),
            w_qk[:, 2048:].reshape(rows, 4, 256),
            w_v.reshape(rows, 4, 256),
            jnp.stack([halves, halves], axis=2).reshape(rows, 4, 1024),
        ],
        axis=2,
    ).transpose(1, 0, 2)


def shards(hidden_in, norm_gain, w_qk, w_v, w_o, prompt_pages, last_fill, page_slots):
    core = lax.axis_index("c")
    role = core * 2 + lax.axis_index("zh")
    y, x = lax.axis_index("y"), lax.axis_index("x")
    quad = (y * 2 + lax.axis_index("zl")) * 4 + x

    slices = role_slices(w_qk, w_v, w_o)
    mine = lax.all_to_all(slices, QUAD, split_axis=0, concat_axis=0, tiled=True)
    level = pair_gather(mine.reshape(64, 2048), "zl")
    query = jnp.stack(ring_pieces(level[:, :, :512], "x"))
    both = jnp.stack(ring_pieces(level[:, :, 512:1024], "y"))

    normed = normalize(after(hidden_in, slices), norm_gain)
    beside = swap(normed, "c")
    across = swap(after(normed, level), "zh")
    diagonal = swap(across, "c")

    offset, live = page_tables(prompt_pages, last_fill, quad * QPAGES)
    sources = page_sources(page_slots, core)
    meta = jnp.concatenate(
        [role[None], offset, live, sources, y[None], x[None]]
    ).astype(jnp.int32)
    cosine, sine = rotation_tables(offset)

    q_parts = ring_pieces(query, "y")
    kv_parts = ring_pieces(both, "x")

    third = after(level[:, :, 1024:], *q_parts, *kv_parts)
    third = jnp.stack(ring_pieces(third, "x"))
    own_half = jnp.stack(ring_pieces(third, "y"))
    other_half = swap(own_half, "c")

    queries, keys, values, halo = [], [], [], []
    for pair, (first, second) in enumerate(((normed, beside), (across, diagonal))):
        q, kvt, v = project(meta, first, second, q_parts, kv_parts, cosine, sine, pair)
        queries.append(q)
        keys.append(kvt)
        values.append(v)
        halo.append(previous_quad(kvt))
    packed = pack(meta, keys, values)
    far = attend(meta, queries[1], keys, halo, 1)
    near = attend(meta, queries[0], keys, halo, 0)
    received = [
        near,
        to_role(far[:TOK], 1),
        to_role(near[TOK:], 2),
        to_role(far[TOK:], 3),
    ]
    attended = output(meta, received, own_half, other_half)
    pages = [packed[0]] + [to_role(packed[flip], flip) for flip in (1, 2, 3)]
    key_cache, value_cache = unpack(meta, pages)
    return (
        attended,
        key_cache.reshape(4, PAGE, 1024),
        value_cache.reshape(4, PAGE, 1024),
    )


def solution(mesh):
    fine = Mesh(mesh.devices.reshape(SIZES), AXES)
    rows = P(AXES, None)
    in_specs = (rows, P(), rows, rows, rows, P(), P(), P(("y", "zl", "x", "c")))
    out_specs = (rows, P(AXES, None, None), P(AXES, None, None))
    return jax.shard_map(
        shards, mesh=fine, in_specs=in_specs, out_specs=out_specs, check_vma=False
    )
```

```python
import functools
import math

import jax
import jax.numpy as jnp
from jax import lax
from jax.experimental import pallas as pl
from jax.experimental.pallas import tpu as pltpu
from jax.sharding import Mesh, PartitionSpec as P


AXES = ("y", "zl", "x", "c", "zh")
SIZES = (4, 2, 4, 2, 2)
QUAD = ("c", "zh")
DEPTH = 2048
TOK = 512
PAGE = 128
QTOK = 4 * TOK
QPAGES = QTOK // PAGE
CHUNK = 256
THETA = 1000000.0
EPS = 1e-05
NEG = -1e30
BF = jnp.bfloat16
INSIDE = pl.BlockSpec(memory_space=pltpu.VMEM)
F32 = jnp.float32


def swap(block, axis):
    return lax.ppermute(block, axis, [(0, 1), (1, 0)])


def shift(block, axis, distance):
    return lax.ppermute(block, axis, [(i, (i + distance) % 4) for i in range(4)])


def to_role(block, flip):
    return lax.ppermute(block, QUAD, [(i, i ^ flip) for i in range(4)])


def ring_pieces(block, axis):
    pieces = [block]
    for distance in (1, 2, 3):
        pieces.append(shift(block, axis, distance))
    return pieces


def slices_kernel(here, qk_ref, v_ref, o_ref, out_ref):
    for role in range(4):
        for copy in (role, role + 4):
            out_ref[copy, :, :512] = qk_ref[:, 512 * role : 512 * role + 512]
            first = 2048 + 256 * role
            out_ref[copy, :, 512:768] = qk_ref[:, first : first + 256]
            out_ref[copy, :, 768:1024] = v_ref[:, 256 * role : 256 * role + 256]
            first = 1024 * (role // 2)
            out_ref[copy, :, 1024:] = o_ref[:, first : first + 1024]


def split_kernel(here, level_ref, kv_ref, rest_ref):
    kv_ref[...] = level_ref[:, :, 512:1024]
    rest_ref[:, :, :512] = level_ref[:, :, :512]
    rest_ref[:, :, 512:] = level_ref[:, :, 1024:]


def arrange_kernel(here, *refs):
    pieces, outs = refs[:4], refs[4:]
    for k in range(4):
        place = lax.rem(here[2] + 4 - k, 4)
        first = 0
        for out_ref in outs:
            width = out_ref.shape[3]
            out_ref[:, place] = pieces[k][:, :, first : first + width]
            first += width


def tick_kernel(in_ref, out_ref):
    for i in range(51):
        out_ref[i] = in_ref[i]


def tick(meta):
    scalars = pl.BlockSpec(memory_space=pltpu.SMEM)
    return pl.pallas_call(
        tick_kernel,
        in_specs=[scalars],
        out_specs=scalars,
        out_shape=jax.ShapeDtypeStruct((51,), jnp.int32),
        name="tick",
    )(meta)


def small(kernel, here, operands, shapes):
    return pl.pallas_call(
        kernel,
        grid_spec=pltpu.PrefetchScalarGridSpec(
            num_scalar_prefetch=1,
            grid=(),
            in_specs=[INSIDE] * len(operands),
            out_specs=[INSIDE] * len(shapes),
        ),
        out_shape=[jax.ShapeDtypeStruct(shape, BF) for shape in shapes],
        compiler_params=pltpu.CompilerParams(vmem_limit_bytes=20 << 20),
    )(here, *operands)


def after(block, *others):
    return lax.optimization_barrier((block, *others))[0]


def normalize(hidden_in, norm_gain):
    values = hidden_in.astype(F32)
    scale = lax.rsqrt(jnp.mean(values * values, axis=-1, keepdims=True) + EPS)
    return (values * scale * norm_gain[None, :]).astype(BF)


def page_tables(prompt_pages, last_fill, first_page):
    count = prompt_pages.shape[0]
    order = jnp.arange(count, dtype=jnp.int32)
    ends = jnp.sum(
        jnp.where(order[None, :] <= order[:, None], prompt_pages[None, :], 0), axis=1
    )
    pages = first_page + jnp.arange(QPAGES, dtype=jnp.int32)
    before = ends[None, :] <= pages[:, None]
    start = jnp.max(jnp.where(before, ends[None, :], 0), axis=1)
    closing = ends[None, :] == pages[:, None] + 1
    short = jnp.sum(jnp.where(closing, PAGE - last_fill[None, :], 0), axis=1)
    return pages - start, PAGE - short


def rotation_tables(offset):
    row = jnp.arange(PAGE, dtype=jnp.int32)
    position = (offset[:, None] * PAGE + row[None, :]).reshape(QTOK)
    half = 64
    freq = jnp.power(THETA, -2.0 * jnp.arange(half, dtype=F32) / 128)
    angle = position.astype(F32)[:, None] * freq[None, :]
    cosine, sine = jnp.cos(angle), jnp.sin(angle)
    return (
        jnp.concatenate([cosine, cosine], axis=-1),
        jnp.concatenate([-sine, sine], axis=-1),
    )


def project_kernel(store, meta, *refs):
    x_refs, parts, tables, out_refs = refs[:2], refs[2:6], refs[6:8], refs[8:]
    step = pl.program_id(0)
    cosine = tables[0][...]
    sine = tables[1][...]

    def turned(block):
        return (block * cosine + pltpu.roll(block, 64, 1) * sine).astype(BF)

    def body(x_ref):
        result = jnp.zeros((x_ref.shape[0], 512), F32)
        for i in range(4):
            start = pl.multiple_of(lax.rem(meta[49] + 4 - i, 4) * 512, 512)
            result += jnp.dot(
                x_ref[:, pl.ds(start, 512)],
                parts[i][...].reshape(512, 512),
                preferred_element_type=F32,
            )
        store(result, turned, *out_refs)

    @pl.when(step < 2)
    def _():
        body(x_refs[0])

    @pl.when(step >= 2)
    def _():
        body(x_refs[1])


def store_queries(result, turned, q_ref):
    for head in range(4):
        lanes = slice(128 * head, 128 * head + 128)
        q_ref[:, lanes] = turned(result[:, lanes])


def store_keys(result, turned, kvt_ref, v_ref):
    for head in range(2):
        kvt_ref[head] = turned(result[:, 128 * head : 128 * head + 128])
        value = result[:, 256 + 128 * head : 384 + 128 * head]
        v_ref[head] = value.astype(BF)
        for page in range(result.shape[0] // PAGE):
            rows = slice(PAGE * page, PAGE * page + PAGE)
            kvt_ref[2 + head, rows, :] = jnp.transpose(value[rows]).astype(BF)


def project(meta, sides, parts, tables, pair, kind):
    tile = 256

    def table(i, m):
        return (jnp.bitwise_xor(m[0], 2 * (i // 2) + pair) * 2 + i % 2, 0)

    if kind == "q":
        store = store_queries
        out_specs = [pl.BlockSpec((tile, 512), lambda i, m: (i, 0))]
        out_shape = [jax.ShapeDtypeStruct((2 * TOK, 512), BF)]
    else:
        store = store_keys
        out_specs = [
            pl.BlockSpec((4, tile, 128), lambda i, m: (0, i, 0)),
            pl.BlockSpec((2, tile, 128), lambda i, m: (0, i, 0)),
        ]
        out_shape = [
            jax.ShapeDtypeStruct((4, 2 * TOK, 128), BF),
            jax.ShapeDtypeStruct((2, 2 * TOK, 128), BF),
        ]
    return pl.pallas_call(
        functools.partial(project_kernel, store),
        grid_spec=pltpu.PrefetchScalarGridSpec(
            num_scalar_prefetch=1,
            grid=(4,),
            in_specs=[
                pl.BlockSpec((tile, DEPTH), lambda i, m: (jnp.minimum(i, 1), 0)),
                pl.BlockSpec((tile, DEPTH), lambda i, m: (jnp.maximum(i - 2, 0), 0)),
            ]
            + [INSIDE] * 4
            + [pl.BlockSpec((tile, 128), table)] * 2,
            out_specs=out_specs,
        ),
        out_shape=out_shape,
        compiler_params=pltpu.CompilerParams(vmem_limit_bytes=40 << 20),
        cost_estimate=pl.CostEstimate(
            flops=4 * TOK * DEPTH * 512, transcendentals=0, bytes_accessed=8 << 20
        ),
    )(meta, *sides, *parts, *tables)


def attend_kernel(pair, meta, *refs):
    q_ref, own, halo, out_ref, kvt, saved, bias = (
        refs[0], refs[1:3], refs[3:5], *refs[5:]
    )
    role = meta[0]
    for p in range(4):
        block = jnp.bitwise_xor(role, 2 * (p % 2) + p // 2)
        source = slice((p % 2) * TOK, (p % 2) * TOK + TOK)
        for at, side in ((0, halo), (4, own)):
            rows = pl.ds(pl.multiple_of((block + at) * TOK, TOK), TOK)
            kvt[:, rows, :] = side[p // 2][:, source, :]
    kvt[:, pl.ds(2 * QTOK, CHUNK), :] = jnp.zeros((4, CHUNK, 128), BF)
    gap = lax.broadcasted_iota(jnp.int32, (CHUNK, 256), 0) - (
        lax.broadcasted_iota(jnp.int32, (CHUNK, 256), 1) % PAGE
    )
    for i in range(2):
        bias[i] = jnp.where(gap <= i * PAGE, 0.0, NEG)
    factor = (1.0 / math.sqrt(128)) * math.log2(math.e)
    tall = lax.broadcasted_iota(jnp.int32, (PAGE, 128), 0)

    def one_page(index, carry):
        rows = pl.ds(pl.multiple_of(index * PAGE, PAGE), PAGE)
        page = jnp.bitwise_xor(role, 2 * (index // 4) + pair) * 4 + index % 4
        offset = meta[1 + page]
        live = meta[17 + page]
        low = QPAGES + page - offset
        full = offset // 2
        stack = [
            jnp.concatenate(
                [
                    q_ref[rows, 256 * h : 256 * h + 128],
                    q_ref[rows, 256 * h + 128 : 256 * h + 256],
                ],
                axis=0,
            )
            for h in range(2)
        ]

        def scan(chunk, tops, count, masked):
            base = pl.multiple_of((low + 2 * chunk) * PAGE, PAGE)
            result = []
            for h in range(2):
                scores = lax.dot_general(
                    kvt[h, pl.ds(base, count * CHUNK), :],
                    stack[h],
                    (((1,), (1,)), ((), ())),
                    preferred_element_type=F32,
                )
                if masked:
                    scores = scores + bias[offset % 2]
                for i in range(count):
                    saved[h, chunk + i] = scores[CHUNK * i : CHUNK * i + CHUNK]
                peak = jnp.max(scores.reshape(count * CHUNK // 8, 8, 256), axis=0)
                result.append(jnp.maximum(tops[h], peak))
            return tuple(result)

        tops = (jnp.full((8, 256), NEG, F32),) * 2
        tops = lax.fori_loop(
            0, full // 2, lambda i, t: scan(2 * i, t, 2, False), tops
        )
        tops = lax.fori_loop(
            full // 2 * 2, full, lambda i, t: scan(i, t, 1, False), tops
        )
        tops = scan(full, tops, 1, True)
        tops = [jnp.max(top, axis=0, keepdims=True) for top in tops]

        def fold(chunk, state, count):
            result = []
            for h in range(2):
                total, acc = state[h]
                parts, weights = [], []
                for i in range(count):
                    expo = jnp.exp2((saved[h, chunk + i] - tops[h]) * factor)
                    total = total + jnp.sum(expo.reshape(CHUNK // 8, 8, 256), axis=0)
                    weights.append(expo.astype(BF))
                for i in range(2 * count):
                    at = pl.multiple_of((low + 2 * chunk + i) * PAGE, PAGE)
                    parts.append(kvt[2 + h, pl.ds(at, PAGE), :])
                acc = acc + jnp.dot(
                    jnp.concatenate(parts, axis=1),
                    jnp.concatenate(weights, axis=0),
                    preferred_element_type=F32,
                )
                result.append((total, acc))
            return tuple(result)

        state = ((jnp.zeros((8, 256), F32), jnp.zeros((128, 256), F32)),) * 2
        count = full + 1
        state = lax.fori_loop(0, count // 2, lambda i, s: fold(2 * i, s, 2), state)
        state = lax.fori_loop(
            count // 2 * 2, count, lambda i, s: fold(i, s, 1), state
        )
        for h in range(2):
            total, acc = state[h]
            value = acc / jnp.sum(total, axis=0, keepdims=True)
            value = jnp.transpose(value)
            for g in range(2):
                part = value[128 * g : 128 * g + 128]
                part = jnp.where(tall < live, part, 0.0)
                at_lane = 256 * h + 128 * g
                out_ref[rows, at_lane : at_lane + 128] = part.astype(BF)
        return carry

    lax.fori_loop(0, 8, one_page, 0)


def attend(meta, queries, own, halo, pair):
    return pl.pallas_call(
        functools.partial(attend_kernel, pair),
        grid_spec=pltpu.PrefetchScalarGridSpec(
            num_scalar_prefetch=1,
            grid=(),
            in_specs=[INSIDE] * 5,
            out_specs=INSIDE,
            scratch_shapes=[
                pltpu.VMEM((4, 2 * QTOK + CHUNK, 128), BF),
                pltpu.VMEM((2, 9, CHUNK, 256), F32),
                pltpu.VMEM((2, CHUNK, 256), F32),
            ],
        ),
        out_shape=jax.ShapeDtypeStruct((2 * TOK, 512), BF),
        compiler_params=pltpu.CompilerParams(vmem_limit_bytes=40 << 20),
        cost_estimate=pl.CostEstimate(
            flops=4 << 30, transcendentals=4 << 20, bytes_accessed=6 << 20
        ),
    )(meta, queries, *own, *halo)


def pack_kernel(meta, *refs):
    keys, values, out_refs, kv = refs[:2], refs[2:4], refs[4:8], refs[8]
    role = meta[0]
    for p in range(4):
        block = jnp.bitwise_xor(role, 2 * (p % 2) + p // 2)
        rows = pl.ds(pl.multiple_of(block * TOK, TOK), TOK)
        source = slice((p % 2) * TOK, (p % 2) * TOK + TOK)
        kv[:2, rows, :] = keys[p // 2][:2, source, :]
        kv[2:, rows, :] = values[p // 2][:, source, :]
    tall = lax.broadcasted_iota(jnp.int32, (PAGE, 128), 0)
    for p in range(4):
        target = jnp.bitwise_xor(role, p)
        for slot in range(4):
            page = meta[33 + target * 4 + slot]
            live = meta[17 + page]
            rows = pl.ds(pl.multiple_of(page * PAGE, PAGE), PAGE)
            for part in range(4):
                block = jnp.where(tall < live, kv[part, rows, :].astype(F32), 0.0)
                lanes = slice(128 * part, 128 * part + 128)
                out_refs[p][PAGE * slot : PAGE * slot + PAGE, lanes] = block.astype(BF)


def pack(meta, keys, values):
    return pl.pallas_call(
        pack_kernel,
        grid_spec=pltpu.PrefetchScalarGridSpec(
            num_scalar_prefetch=1,
            grid=(),
            in_specs=[INSIDE] * 4,
            out_specs=[INSIDE] * 4,
            scratch_shapes=[pltpu.VMEM((4, QTOK, 128), BF)],
        ),
        out_shape=[jax.ShapeDtypeStruct((TOK, 512), BF)] * 4,
        compiler_params=pltpu.CompilerParams(vmem_limit_bytes=30 << 20),
        name="pack_pages",
    )(meta, *keys, *values)


def unpack_kernel(meta, *refs):
    in_refs, key_ref, value_ref = refs[:4], refs[4], refs[5]
    step = pl.program_id(0)
    for p in range(4):

        @pl.when(step == p)
        def _(p=p):
            key_ref[...] = in_refs[p][:, :256]
            value_ref[...] = in_refs[p][:, 256:]


def unpack(meta, received):
    whole = pl.BlockSpec((TOK, 512), lambda i, m: (0, 0))
    column = pl.BlockSpec((TOK, 256), lambda i, m: (0, jnp.bitwise_xor(m[0], i)))
    return pl.pallas_call(
        unpack_kernel,
        grid_spec=pltpu.PrefetchScalarGridSpec(
            num_scalar_prefetch=1,
            grid=(4,),
            in_specs=[whole] * 4,
            out_specs=[column] * 2,
        ),
        out_shape=[jax.ShapeDtypeStruct((TOK, 1024), BF)] * 2,
        compiler_params=pltpu.CompilerParams(vmem_limit_bytes=30 << 20),
        name="unpack_pages",
    )(meta, *received)


def output_kernel(meta, *refs):
    in_refs, weights, out_ref = refs[:4], refs[4:6], refs[6]
    step = pl.program_id(0)
    for half in range(2):

        @pl.when(step == half)
        def _(half=half):
            total = jnp.zeros((TOK, 1024), F32)
            for p in range(4):
                block = jnp.bitwise_xor(meta[0], p)
                total += jnp.dot(
                    in_refs[p][...],
                    weights[half][lax.rem(meta[49] + 4 - block, 4)].reshape(512, 1024),
                    preferred_element_type=F32,
                )
            out_ref[...] = total.astype(BF)


def output(meta, received, own_half, other_half):
    whole = pl.BlockSpec((TOK, 512), lambda i, m: (0, 0))
    return pl.pallas_call(
        output_kernel,
        grid_spec=pltpu.PrefetchScalarGridSpec(
            num_scalar_prefetch=1,
            grid=(2,),
            in_specs=[whole] * 4 + [INSIDE] * 2,
            out_specs=pl.BlockSpec(
                (TOK, 1024), lambda i, m: (0, jnp.bitwise_xor(m[0] // 2, i))
            ),
        ),
        out_shape=jax.ShapeDtypeStruct((TOK, DEPTH), BF),
        compiler_params=pltpu.CompilerParams(vmem_limit_bytes=48 << 20),
        name="output_rows",
    )(meta, *received, own_half, other_half)


def page_sources(page_slots, core):
    other = swap(page_slots, "c")
    first = jnp.where(core == 0, page_slots, other)
    second = jnp.where(core == 0, other, page_slots)
    slots = jnp.stack([first, second])
    wanted = jnp.arange(8, dtype=jnp.int32)
    hit = slots[:, None, :] == wanted[None, :, None]
    found = jnp.sum(jnp.where(hit, wanted[None, None, :], 0), axis=2)
    return (found + jnp.array([[0], [8]], jnp.int32)).reshape(16)


def previous_quad(block):
    names = ("y", "zl", "x", "c", "zh")
    route = [(i, i + 4) for i in range(124)]
    return lax.ppermute(block, names, route)


def shards(hidden_in, norm_gain, w_qk, w_v, w_o, prompt_pages, last_fill, page_slots):
    core = lax.axis_index("c")
    role = core * 2 + lax.axis_index("zh")
    y, x = lax.axis_index("y"), lax.axis_index("x")
    quad = (y * 2 + lax.axis_index("zl")) * 4 + x

    here = jnp.stack([role, y, x]).astype(jnp.int32)

    slices = small(slices_kernel, here, (w_qk, w_v, w_o), [(8, 16, 2048)])[0]
    level = lax.all_to_all(
        slices, ("zl", "c", "zh"), split_axis=0, concat_axis=0, tiled=True
    ).reshape(2, 64, 2048)
    kv_level, rest = small(split_kernel, here, (level,), [(2, 64, 512), (2, 64, 1536)])
    kv_row = small(
        arrange_kernel, here, ring_pieces(kv_level, "x"), [(2, 4, 64, 512)]
    )[0]
    kv_parts = ring_pieces(kv_row, "y")
    q_row, o_row = small(
        arrange_kernel,
        here,
        ring_pieces(after(rest, kv_row), "x"),
        [(2, 4, 64, 512), (2, 4, 64, 1024)],
    )
    q_parts = ring_pieces(q_row, "y")
    o_parts = ring_pieces(o_row, "y")

    normed = normalize(after(hidden_in, slices), norm_gain)
    beside = swap(normed, "c")
    across = swap(after(normed, level), "zh")
    diagonal = swap(across, "c")

    offset, live = page_tables(prompt_pages, last_fill, quad * QPAGES)
    sources = page_sources(page_slots, core)
    meta = jnp.concatenate(
        [role[None], offset, live, sources, y[None], x[None]]
    ).astype(jnp.int32)
    tables = rotation_tables(offset)

    sides = ((normed, beside), (across, diagonal))
    keys, values, halo, queries = [], [], [], []
    for pair in range(2):
        kvt, v = project(meta, sides[pair], kv_parts, tables, pair, "kv")
        keys.append(kvt)
        values.append(v)
        halo.append(previous_quad(kvt))
    later = after(tick(meta), *keys)
    for pair in range(2):
        queries += project(later, sides[pair], q_parts, tables, pair, "q")
    packed = pack(meta, keys, values)
    pages = [packed[0]]
    for flip in (1, 2, 3):
        pages.append(to_role(packed[flip], flip))

    far = attend(meta, queries[1], keys, halo, 1)
    far = swap(far, "zh")
    near = attend(meta, queries[0], keys, halo, 0)
    own_half = jnp.stack(o_parts)
    other_half = swap(own_half, "c")
    received = [near, far, swap(near[TOK:], "c"), swap(far[TOK:], "c")]
    attended = output(meta, received, own_half, other_half)
    key_cache, value_cache = unpack(meta, pages)
    return (
        attended,
        key_cache.reshape(4, PAGE, 1024),
        value_cache.reshape(4, PAGE, 1024),
    )


def solution(mesh):
    fine = Mesh(mesh.devices.reshape(SIZES), AXES)
    rows = P(AXES, None)
    in_specs = (rows, P(), rows, rows, rows, P(), P(), P(("y", "zl", "x", "c")))
    out_specs = (rows, P(AXES, None, None), P(AXES, None, None))
    return jax.shard_map(
        shards, mesh=fine, in_specs=in_specs, out_specs=out_specs, check_vma=False
    )
```

```python
import functools
import math

import jax
import jax.numpy as jnp
from jax import lax
from jax.experimental import pallas as pl
from jax.experimental.pallas import tpu as pltpu
from jax.sharding import Mesh, PartitionSpec as P


AXES = ("y", "zl", "x", "c", "zh")
SIZES = (4, 2, 4, 2, 2)
QUAD = ("c", "zh")
DEPTH = 2048
TOK = 512
PAGE = 128
QTOK = 4 * TOK
QPAGES = QTOK // PAGE
CHUNK = 256
THETA = 1000000.0
EPS = 1e-05
NEG = -1e30
BF = jnp.bfloat16
INSIDE = pl.BlockSpec(memory_space=pltpu.VMEM)
F32 = jnp.float32


def swap(block, axis):
    return lax.ppermute(block, axis, [(0, 1), (1, 0)])


def shift(block, axis, distance):
    return lax.ppermute(block, axis, [(i, (i + distance) % 4) for i in range(4)])


def to_role(block, flip):
    return lax.ppermute(block, QUAD, [(i, i ^ flip) for i in range(4)])


def ring_pieces(block, axis):
    pieces = [block]
    for distance in (1, 2, 3):
        pieces.append(shift(block, axis, distance))
    return pieces


def ring_chain(block, axis):
    pieces = [block]
    for _ in range(3):
        pieces.append(shift(pieces[-1], axis, -1))
    return pieces


def slices_kernel(here, qk_ref, v_ref, o_ref, out_ref):
    for role in range(4):
        for copy in (role, role + 4):
            out_ref[copy, :, :512] = qk_ref[:, 512 * role : 512 * role + 512]
            first = 2048 + 256 * role
            out_ref[copy, :, 512:768] = qk_ref[:, first : first + 256]
            out_ref[copy, :, 768:1024] = v_ref[:, 256 * role : 256 * role + 256]
            first = 1024 * (role // 2)
            out_ref[copy, :, 1024:] = o_ref[:, first : first + 1024]


def split_kernel(here, level_ref, kv_ref, rest_ref):
    kv_ref[...] = level_ref[:, :, 512:1024]
    rest_ref[:, :, :512] = level_ref[:, :, :512]
    rest_ref[:, :, 512:] = level_ref[:, :, 1024:]


def arrange_kernel(here, *refs):
    pieces, outs = refs[:4], refs[4:]
    for k in range(4):
        place = lax.rem(here[2] + 4 - k, 4)
        first = 0
        for out_ref in outs:
            width = out_ref.shape[3]
            out_ref[:, place] = pieces[k][:, :, first : first + width]
            first += width


def column_kernel(here, *refs):
    for k in range(4):
        refs[4][lax.rem(here[1] + 4 - k, 4)] = refs[k][...]


def tick_kernel(in_ref, out_ref):
    for i in range(51):
        out_ref[i] = in_ref[i]


def tick(meta):
    scalars = pl.BlockSpec(memory_space=pltpu.SMEM)
    return pl.pallas_call(
        tick_kernel,
        in_specs=[scalars],
        out_specs=scalars,
        out_shape=jax.ShapeDtypeStruct((51,), jnp.int32),
        name="tick",
    )(meta)


def small(kernel, here, operands, shapes):
    return pl.pallas_call(
        kernel,
        grid_spec=pltpu.PrefetchScalarGridSpec(
            num_scalar_prefetch=1,
            grid=(),
            in_specs=[INSIDE] * len(operands),
            out_specs=[INSIDE] * len(shapes),
        ),
        out_shape=[jax.ShapeDtypeStruct(shape, BF) for shape in shapes],
        compiler_params=pltpu.CompilerParams(vmem_limit_bytes=20 << 20),
    )(here, *operands)


def after(block, *others):
    return lax.optimization_barrier((block, *others))[0]


def normalize(hidden_in, norm_gain):
    values = hidden_in.astype(F32)
    scale = lax.rsqrt(jnp.mean(values * values, axis=-1, keepdims=True) + EPS)
    return (values * scale * norm_gain[None, :]).astype(BF)


def page_tables(prompt_pages, last_fill, first_page):
    count = prompt_pages.shape[0]
    order = jnp.arange(count, dtype=jnp.int32)
    ends = jnp.sum(
        jnp.where(order[None, :] <= order[:, None], prompt_pages[None, :], 0), axis=1
    )
    pages = first_page + jnp.arange(QPAGES, dtype=jnp.int32)
    before = ends[None, :] <= pages[:, None]
    start = jnp.max(jnp.where(before, ends[None, :], 0), axis=1)
    closing = ends[None, :] == pages[:, None] + 1
    short = jnp.sum(jnp.where(closing, PAGE - last_fill[None, :], 0), axis=1)
    return pages - start, PAGE - short


def rotation_tables(offset):
    row = jnp.arange(PAGE, dtype=jnp.int32)
    position = (offset[:, None] * PAGE + row[None, :]).reshape(QTOK)
    half = 64
    freq = jnp.power(THETA, -2.0 * jnp.arange(half, dtype=F32) / 128)
    angle = position.astype(F32)[:, None] * freq[None, :]
    cosine, sine = jnp.cos(angle), jnp.sin(angle)
    return (
        jnp.concatenate([cosine, cosine], axis=-1),
        jnp.concatenate([-sine, sine], axis=-1),
    )


def project_kernel(store, meta, *refs):
    x_refs, parts, tables, out_refs = refs[:2], refs[2:6], refs[6:8], refs[8:]
    if store is store_keys:
        out_refs, weight = out_refs[:-1], out_refs[-1]
    step = pl.program_id(0)
    cosine = tables[0][...]
    sine = tables[1][...]

    def turned(block):
        return (block * cosine + pltpu.roll(block, 64, 1) * sine).astype(BF)

    if store is store_keys:

        @pl.when(step == 0)
        def _():
            for i in range(4):
                weight[:, :, lax.rem(meta[50] + 4 - i, 4)] = parts[i][...]

    def body(x_ref):
        if store is store_keys:
            result = jnp.dot(
                x_ref[...],
                weight[...].reshape(DEPTH, 512),
                preferred_element_type=F32,
            )
        else:
            result = jnp.zeros((x_ref.shape[0], 512), F32)
            for i in range(4):
                start = pl.multiple_of(lax.rem(meta[49] + 4 - i, 4) * 512, 512)
                result += jnp.dot(
                    x_ref[:, pl.ds(start, 512)],
                    parts[i][...].reshape(512, 512),
                    preferred_element_type=F32,
                )
        store(result, turned, *out_refs)

    @pl.when(step < 2)
    def _():
        body(x_refs[0])

    @pl.when(step >= 2)
    def _():
        body(x_refs[1])


def store_queries(result, turned, q_ref):
    for head in range(4):
        lanes = slice(128 * head, 128 * head + 128)
        q_ref[:, lanes] = turned(result[:, lanes])


def store_keys(result, turned, kvt_ref, v_ref):
    for head in range(2):
        kvt_ref[head] = turned(result[:, 128 * head : 128 * head + 128])
        value = result[:, 256 + 128 * head : 384 + 128 * head]
        v_ref[head] = value.astype(BF)
        for page in range(result.shape[0] // PAGE):
            rows = slice(PAGE * page, PAGE * page + PAGE)
            kvt_ref[2 + head, rows, :] = jnp.transpose(value[rows]).astype(BF)


def project(meta, sides, parts, tables, pair, kind):
    tile = 256

    def table(i, m):
        return (jnp.bitwise_xor(m[0], 2 * (i // 2) + pair) * 2 + i % 2, 0)

    if kind == "q":
        store = store_queries
        scratch = []
        out_specs = [pl.BlockSpec((tile, 512), lambda i, m: (i, 0))]
        out_shape = [jax.ShapeDtypeStruct((2 * TOK, 512), BF)]
    else:
        store = store_keys
        scratch = [pltpu.VMEM((4, 2, 4, 64, 512), BF)]
        out_specs = [
            pl.BlockSpec((4, tile, 128), lambda i, m: (0, i, 0)),
            pl.BlockSpec((2, tile, 128), lambda i, m: (0, i, 0)),
        ]
        out_shape = [
            jax.ShapeDtypeStruct((4, 2 * TOK, 128), BF),
            jax.ShapeDtypeStruct((2, 2 * TOK, 128), BF),
        ]
    return pl.pallas_call(
        functools.partial(project_kernel, store),
        grid_spec=pltpu.PrefetchScalarGridSpec(
            num_scalar_prefetch=1,
            grid=(4,),
            in_specs=[
                pl.BlockSpec((tile, DEPTH), lambda i, m: (jnp.minimum(i, 1), 0)),
                pl.BlockSpec((tile, DEPTH), lambda i, m: (jnp.maximum(i - 2, 0), 0)),
            ]
            + [INSIDE] * 4
            + [pl.BlockSpec((tile, 128), table)] * 2,
            out_specs=out_specs,
            scratch_shapes=scratch,
        ),
        out_shape=out_shape,
        compiler_params=pltpu.CompilerParams(vmem_limit_bytes=40 << 20),
        cost_estimate=pl.CostEstimate(
            flops=4 * TOK * DEPTH * 512, transcendentals=0, bytes_accessed=8 << 20
        ),
    )(meta, *sides, *parts, *tables)


def attend_kernel(pair, meta, *refs):
    q_ref, own, halo, out_ref, kvt, saved, bias = (
        refs[0], refs[1:3], refs[3:5], *refs[5:]
    )
    role = meta[0]
    for p in range(4):
        block = jnp.bitwise_xor(role, 2 * (p % 2) + p // 2)
        source = slice((p % 2) * TOK, (p % 2) * TOK + TOK)
        for at, side in ((0, halo), (4, own)):
            rows = pl.ds(pl.multiple_of((block + at) * TOK, TOK), TOK)
            kvt[:, rows, :] = side[p // 2][:, source, :]
    kvt[:, pl.ds(2 * QTOK, CHUNK), :] = jnp.zeros((4, CHUNK, 128), BF)
    gap = lax.broadcasted_iota(jnp.int32, (CHUNK, 256), 0) - (
        lax.broadcasted_iota(jnp.int32, (CHUNK, 256), 1) % PAGE
    )
    for i in range(2):
        bias[i] = jnp.where(gap <= i * PAGE, 0.0, NEG)
    factor = (1.0 / math.sqrt(128)) * math.log2(math.e)
    tall = lax.broadcasted_iota(jnp.int32, (PAGE, 128), 0)

    def one_page(index, carry):
        rows = pl.ds(pl.multiple_of(index * PAGE, PAGE), PAGE)
        page = jnp.bitwise_xor(role, 2 * (index // 4) + pair) * 4 + index % 4
        offset = meta[1 + page]
        live = meta[17 + page]
        low = QPAGES + page - offset
        full = offset // 2
        stack = [
            jnp.concatenate(
                [
                    q_ref[rows, 256 * h : 256 * h + 128],
                    q_ref[rows, 256 * h + 128 : 256 * h + 256],
                ],
                axis=0,
            )
            for h in range(2)
        ]

        def scan(chunk, tops, count, masked):
            base = pl.multiple_of((low + 2 * chunk) * PAGE, PAGE)
            result = []
            for h in range(2):
                scores = lax.dot_general(
                    kvt[h, pl.ds(base, count * CHUNK), :],
                    stack[h],
                    (((1,), (1,)), ((), ())),
                    preferred_element_type=F32,
                )
                if masked:
                    scores = scores + bias[offset % 2]
                for i in range(count):
                    saved[h, chunk + i] = scores[CHUNK * i : CHUNK * i + CHUNK]
                peak = jnp.max(scores.reshape(count * CHUNK // 8, 8, 256), axis=0)
                result.append(jnp.maximum(tops[h], peak))
            return tuple(result)

        tops = (jnp.full((8, 256), NEG, F32),) * 2
        tops = lax.fori_loop(
            0, full // 2, lambda i, t: scan(2 * i, t, 2, False), tops
        )
        tops = lax.fori_loop(
            full // 2 * 2, full, lambda i, t: scan(i, t, 1, False), tops
        )
        tops = scan(full, tops, 1, True)
        tops = [jnp.max(top, axis=0, keepdims=True) for top in tops]

        def fold(chunk, state, count):
            result = []
            for h in range(2):
                total, acc = state[h]
                parts, weights = [], []
                for i in range(count):
                    expo = jnp.exp2((saved[h, chunk + i] - tops[h]) * factor)
                    total = total + jnp.sum(expo.reshape(CHUNK // 8, 8, 256), axis=0)
                    weights.append(expo.astype(BF))
                for i in range(2 * count):
                    at = pl.multiple_of((low + 2 * chunk + i) * PAGE, PAGE)
                    parts.append(kvt[2 + h, pl.ds(at, PAGE), :])
                acc = acc + jnp.dot(
                    jnp.concatenate(parts, axis=1),
                    jnp.concatenate(weights, axis=0),
                    preferred_element_type=F32,
                )
                result.append((total, acc))
            return tuple(result)

        state = ((jnp.zeros((8, 256), F32), jnp.zeros((128, 256), F32)),) * 2
        count = full + 1
        state = lax.fori_loop(0, count // 2, lambda i, s: fold(2 * i, s, 2), state)
        state = lax.fori_loop(
            count // 2 * 2, count, lambda i, s: fold(i, s, 1), state
        )
        for h in range(2):
            total, acc = state[h]
            value = acc / jnp.sum(total, axis=0, keepdims=True)
            value = jnp.transpose(value)
            for g in range(2):
                part = value[128 * g : 128 * g + 128]
                part = jnp.where(tall < live, part, 0.0)
                at_lane = 256 * h + 128 * g
                out_ref[rows, at_lane : at_lane + 128] = part.astype(BF)
        return carry

    lax.fori_loop(0, 8, one_page, 0)


def attend(meta, queries, own, halo, pair):
    return pl.pallas_call(
        functools.partial(attend_kernel, pair),
        grid_spec=pltpu.PrefetchScalarGridSpec(
            num_scalar_prefetch=1,
            grid=(),
            in_specs=[INSIDE] * 5,
            out_specs=INSIDE,
            scratch_shapes=[
                pltpu.VMEM((4, 2 * QTOK + CHUNK, 128), BF),
                pltpu.VMEM((2, 9, CHUNK, 256), F32),
                pltpu.VMEM((2, CHUNK, 256), F32),
            ],
        ),
        out_shape=jax.ShapeDtypeStruct((2 * TOK, 512), BF),
        compiler_params=pltpu.CompilerParams(vmem_limit_bytes=40 << 20),
        cost_estimate=pl.CostEstimate(
            flops=4 << 30, transcendentals=4 << 20, bytes_accessed=6 << 20
        ),
    )(meta, queries, *own, *halo)


def pack_kernel(meta, *refs):
    keys, values, out_refs, kv = refs[:2], refs[2:4], refs[4:8], refs[8]
    role = meta[0]
    for p in range(4):
        block = jnp.bitwise_xor(role, 2 * (p % 2) + p // 2)
        rows = pl.ds(pl.multiple_of(block * TOK, TOK), TOK)
        source = slice((p % 2) * TOK, (p % 2) * TOK + TOK)
        kv[:2, rows, :] = keys[p // 2][:2, source, :]
        kv[2:, rows, :] = values[p // 2][:, source, :]
    tall = lax.broadcasted_iota(jnp.int32, (PAGE, 128), 0)
    for p in range(4):
        target = jnp.bitwise_xor(role, p)
        for slot in range(4):
            page = meta[33 + target * 4 + slot]
            live = meta[17 + page]
            rows = pl.ds(pl.multiple_of(page * PAGE, PAGE), PAGE)
            for part in range(4):
                block = jnp.where(tall < live, kv[part, rows, :].astype(F32), 0.0)
                lanes = slice(128 * part, 128 * part + 128)
                out_refs[p][PAGE * slot : PAGE * slot + PAGE, lanes] = block.astype(BF)


def pack(meta, keys, values):
    return pl.pallas_call(
        pack_kernel,
        grid_spec=pltpu.PrefetchScalarGridSpec(
            num_scalar_prefetch=1,
            grid=(),
            in_specs=[INSIDE] * 4,
            out_specs=[INSIDE] * 4,
            scratch_shapes=[pltpu.VMEM((4, QTOK, 128), BF)],
        ),
        out_shape=[jax.ShapeDtypeStruct((TOK, 512), BF)] * 4,
        compiler_params=pltpu.CompilerParams(vmem_limit_bytes=30 << 20),
        name="pack_pages",
    )(meta, *keys, *values)


def unpack_kernel(meta, *refs):
    in_refs, key_ref, value_ref = refs[:4], refs[4], refs[5]
    step = pl.program_id(0)
    for p in range(4):

        @pl.when(step == p)
        def _(p=p):
            key_ref[...] = in_refs[p][:, :256]
            value_ref[...] = in_refs[p][:, 256:]


def unpack(meta, received):
    whole = pl.BlockSpec((TOK, 512), lambda i, m: (0, 0))
    column = pl.BlockSpec((TOK, 256), lambda i, m: (0, jnp.bitwise_xor(m[0], i)))
    return pl.pallas_call(
        unpack_kernel,
        grid_spec=pltpu.PrefetchScalarGridSpec(
            num_scalar_prefetch=1,
            grid=(4,),
            in_specs=[whole] * 4,
            out_specs=[column] * 2,
        ),
        out_shape=[jax.ShapeDtypeStruct((TOK, 1024), BF)] * 2,
        compiler_params=pltpu.CompilerParams(vmem_limit_bytes=30 << 20),
        name="unpack_pages",
    )(meta, *received)


def fill_rows(meta, parts, weight, parity):
    for half in range(2):
        for d in range(4):
            flip = jnp.bitwise_xor(lax.rem(meta[49] + d, 4), meta[0])

            @pl.when(lax.rem(flip, 2) == parity)
            def _(half=half, d=d, flip=flip):
                weight[half, flip // 2] = parts[4 * half + d][...].reshape(512, 1024)


def pair_product(in_refs, weight, half):
    return jnp.dot(
        in_refs[0][:TOK], weight[half, 0], preferred_element_type=F32
    ) + jnp.dot(in_refs[1][...], weight[half, 1], preferred_element_type=F32)


def near_kernel(meta, *refs):
    in_refs, parts, out_ref, weight = refs[:2], refs[2:10], refs[10], refs[11]
    fill_rows(meta, parts, weight, 0)
    for half in range(2):
        out_ref[half] = pair_product(in_refs, weight, half)


def far_kernel(meta, *refs):
    in_refs, parts, partial, out_ref, weight = (
        refs[:2], refs[2:10], refs[10], refs[11], refs[12]
    )
    step = pl.program_id(0)

    @pl.when(step == 0)
    def _():
        fill_rows(meta, parts, weight, 1)

    for half in range(2):

        @pl.when(step == half)
        def _(half=half):
            total = partial[half] + pair_product(in_refs, weight, half)
            out_ref[...] = total.astype(BF)


def output_near(meta, pair, parts):
    return pl.pallas_call(
        near_kernel,
        grid_spec=pltpu.PrefetchScalarGridSpec(
            num_scalar_prefetch=1,
            grid=(),
            in_specs=[INSIDE] * 10,
            out_specs=INSIDE,
            scratch_shapes=[pltpu.VMEM((2, 2, 512, 1024), BF)],
        ),
        out_shape=jax.ShapeDtypeStruct((2, TOK, 1024), F32),
        compiler_params=pltpu.CompilerParams(vmem_limit_bytes=32 << 20),
        name="output_near",
    )(meta, *pair, *parts)


def output_far(meta, pair, parts, partial):
    return pl.pallas_call(
        far_kernel,
        grid_spec=pltpu.PrefetchScalarGridSpec(
            num_scalar_prefetch=1,
            grid=(2,),
            in_specs=[INSIDE] * 11,
            out_specs=pl.BlockSpec(
                (TOK, 1024), lambda i, m: (0, jnp.bitwise_xor(m[0] // 2, i))
            ),
            scratch_shapes=[pltpu.VMEM((2, 2, 512, 1024), BF)],
        ),
        out_shape=jax.ShapeDtypeStruct((TOK, DEPTH), BF),
        compiler_params=pltpu.CompilerParams(vmem_limit_bytes=32 << 20),
        name="output_far",
    )(meta, *pair, *parts, partial)


def page_sources(page_slots, core):
    other = swap(page_slots, "c")
    first = jnp.where(core == 0, page_slots, other)
    second = jnp.where(core == 0, other, page_slots)
    slots = jnp.stack([first, second])
    wanted = jnp.arange(8, dtype=jnp.int32)
    hit = slots[:, None, :] == wanted[None, :, None]
    found = jnp.sum(jnp.where(hit, wanted[None, None, :], 0), axis=2)
    return (found + jnp.array([[0], [8]], jnp.int32)).reshape(16)


def previous_quad(block):
    names = ("y", "zl", "x", "c", "zh")
    route = [(i, i + 4) for i in range(124)]
    return lax.ppermute(block, names, route)


def shards(hidden_in, norm_gain, w_qk, w_v, w_o, prompt_pages, last_fill, page_slots):
    core = lax.axis_index("c")
    role = core * 2 + lax.axis_index("zh")
    y, x = lax.axis_index("y"), lax.axis_index("x")
    quad = (y * 2 + lax.axis_index("zl")) * 4 + x

    here = jnp.stack([role, y, x]).astype(jnp.int32)

    slices = small(slices_kernel, here, (w_qk, w_v, w_o), [(8, 16, 2048)])[0]
    level = lax.all_to_all(
        slices, ("zl", "c", "zh"), split_axis=0, concat_axis=0, tiled=True
    ).reshape(2, 64, 2048)
    kv_level, rest = small(split_kernel, here, (level,), [(2, 64, 512), (2, 64, 1536)])
    kv_row = small(
        column_kernel, here, ring_pieces(kv_level, "y"), [(4, 2, 64, 512)]
    )[0]
    kv_parts = ring_pieces(kv_row, "x")
    q_row, o_row = small(
        arrange_kernel,
        here,
        ring_pieces(after(rest, kv_row), "x"),
        [(2, 4, 64, 512), (2, 4, 64, 1024)],
    )
    q_parts = ring_pieces(q_row, "y")
    o_parts = ring_chain(o_row, "y")

    normed = normalize(after(hidden_in, slices), norm_gain)
    beside = swap(normed, "c")
    across = swap(after(normed, level), "zh")
    diagonal = swap(across, "c")

    offset, live = page_tables(prompt_pages, last_fill, quad * QPAGES)
    sources = page_sources(page_slots, core)
    meta = jnp.concatenate(
        [role[None], offset, live, sources, y[None], x[None]]
    ).astype(jnp.int32)
    tables = rotation_tables(offset)

    sides = ((normed, beside), (across, diagonal))
    keys, values, halo, queries = [], [], [], []
    for pair in range(2):
        kvt, v = project(meta, sides[pair], kv_parts, tables, pair, "kv")
        keys.append(kvt)
        values.append(v)
        halo.append(previous_quad(kvt))
    later = after(tick(meta), *keys)
    for pair in range(2):
        queries += project(later, sides[pair], q_parts, tables, pair, "q")
    packed = pack(meta, keys, values)
    pages = [packed[0]]
    for flip in (1, 2, 3):
        pages.append(to_role(packed[flip], flip))

    far = attend(meta, queries[1], keys, halo, 1)
    far = swap(far, "zh")
    near = attend(meta, queries[0], keys, halo, 0)
    o_parts = list(o_parts)
    for i in range(4):
        o_parts.append(swap(o_parts[i], "c"))
    partial = output_near(meta, (near, swap(near[TOK:], "c")), o_parts)
    diagonal_far = swap(far[TOK:], "c")
    attended = output_far(meta, (far, diagonal_far), o_parts, partial)
    key_cache, value_cache = unpack(meta, pages)
    return (
        attended,
        key_cache.reshape(4, PAGE, 1024),
        value_cache.reshape(4, PAGE, 1024),
    )


def solution(mesh):
    fine = Mesh(mesh.devices.reshape(SIZES), AXES)
    rows = P(AXES, None)
    in_specs = (rows, P(), rows, rows, rows, P(), P(), P(("y", "zl", "x", "c")))
    out_specs = (rows, P(AXES, None, None), P(AXES, None, None))
    return jax.shard_map(
        shards, mesh=fine, in_specs=in_specs, out_specs=out_specs, check_vma=False
    )
```

```python
import functools
import math

import jax
import jax.numpy as jnp
from jax import lax
from jax.experimental import pallas as pl
from jax.experimental.pallas import tpu as pltpu
from jax.sharding import Mesh, PartitionSpec as P


AXES = ("y", "zl", "x", "c", "zh")
SIZES = (4, 2, 4, 2, 2)
QUAD = ("c", "zh")
DEPTH = 2048
TOK = 512
PAGE = 128
QTOK = 4 * TOK
QPAGES = QTOK // PAGE
CHUNK = 256
THETA = 1000000.0
EPS = 1e-05
NEG = -1e30
BF = jnp.bfloat16
INSIDE = pl.BlockSpec(memory_space=pltpu.VMEM)
F32 = jnp.float32


def swap(block, axis):
    return lax.ppermute(block, axis, [(0, 1), (1, 0)])


def shift(block, axis, distance):
    return lax.ppermute(block, axis, [(i, (i + distance) % 4) for i in range(4)])


def to_role(block, flip):
    return lax.ppermute(block, QUAD, [(i, i ^ flip) for i in range(4)])


def ring_pieces(block, axis):
    pieces = [block]
    for distance in (1, 2, 3):
        pieces.append(shift(block, axis, distance))
    return pieces


def ring_chain(block, axis):
    pieces = [block]
    for _ in range(3):
        pieces.append(shift(pieces[-1], axis, -1))
    return pieces


def slices_kernel(here, qk_ref, v_ref, o_ref, out_ref):
    for role in range(4):
        for copy in (role, role + 4):
            out_ref[copy, :, :512] = qk_ref[:, 512 * role : 512 * role + 512]
            first = 2048 + 256 * role
            out_ref[copy, :, 512:768] = qk_ref[:, first : first + 256]
            out_ref[copy, :, 768:1024] = v_ref[:, 256 * role : 256 * role + 256]
            first = 1024 * (role // 2)
            out_ref[copy, :, 1024:] = o_ref[:, first : first + 1024]


def split_kernel(here, level_ref, kv_ref, q_ref, o_ref):
    kv_ref[...] = level_ref[:, :, 512:1024]
    q_ref[...] = level_ref[:, :, :512]
    o_ref[...] = level_ref[:, :, 1024:]


def arrange_kernel(here, *refs):
    pieces, outs = refs[:4], refs[4:]
    for k in range(4):
        place = lax.rem(here[2] + 4 - k, 4)
        first = 0
        for out_ref in outs:
            width = out_ref.shape[3]
            out_ref[:, place] = pieces[k][:, :, first : first + width]
            first += width


def column_kernel(here, *refs):
    for k in range(4):
        refs[4][lax.rem(here[1] + 4 - k, 4)] = refs[k][...]


def tick_kernel(in_ref, out_ref):
    for i in range(51):
        out_ref[i] = in_ref[i]


def tick(meta):
    scalars = pl.BlockSpec(memory_space=pltpu.SMEM)
    return pl.pallas_call(
        tick_kernel,
        in_specs=[scalars],
        out_specs=scalars,
        out_shape=jax.ShapeDtypeStruct((51,), jnp.int32),
        name="tick",
    )(meta)


def small(kernel, here, operands, shapes):
    return pl.pallas_call(
        kernel,
        grid_spec=pltpu.PrefetchScalarGridSpec(
            num_scalar_prefetch=1,
            grid=(),
            in_specs=[INSIDE] * len(operands),
            out_specs=[INSIDE] * len(shapes),
        ),
        out_shape=[jax.ShapeDtypeStruct(shape, BF) for shape in shapes],
        compiler_params=pltpu.CompilerParams(vmem_limit_bytes=20 << 20),
    )(here, *operands)


def after(block, *others):
    return lax.optimization_barrier((block, *others))[0]


def normalize(hidden_in, norm_gain):
    values = hidden_in.astype(F32)
    scale = lax.rsqrt(jnp.mean(values * values, axis=-1, keepdims=True) + EPS)
    return (values * scale * norm_gain[None, :]).astype(BF)


def page_tables(prompt_pages, last_fill, first_page):
    count = prompt_pages.shape[0]
    order = jnp.arange(count, dtype=jnp.int32)
    ends = jnp.sum(
        jnp.where(order[None, :] <= order[:, None], prompt_pages[None, :], 0), axis=1
    )
    pages = first_page + jnp.arange(QPAGES, dtype=jnp.int32)
    before = ends[None, :] <= pages[:, None]
    start = jnp.max(jnp.where(before, ends[None, :], 0), axis=1)
    closing = ends[None, :] == pages[:, None] + 1
    short = jnp.sum(jnp.where(closing, PAGE - last_fill[None, :], 0), axis=1)
    return pages - start, PAGE - short


def rotation_tables(offset):
    row = jnp.arange(PAGE, dtype=jnp.int32)
    position = (offset[:, None] * PAGE + row[None, :]).reshape(QTOK)
    half = 64
    freq = jnp.power(THETA, -2.0 * jnp.arange(half, dtype=F32) / 128)
    angle = position.astype(F32)[:, None] * freq[None, :]
    cosine, sine = jnp.cos(angle), jnp.sin(angle)
    return (
        jnp.concatenate([cosine, cosine], axis=-1),
        jnp.concatenate([-sine, sine], axis=-1),
    )


def project_kernel(store, meta, *refs):
    x_refs, parts, tables, out_refs = refs[:2], refs[2:6], refs[6:8], refs[8:]
    if store is store_keys:
        out_refs, weight = out_refs[:-1], out_refs[-1]
    step = pl.program_id(0)
    cosine = tables[0][...]
    sine = tables[1][...]

    def turned(block):
        return (block * cosine + pltpu.roll(block, 64, 1) * sine).astype(BF)

    if store is store_keys:

        @pl.when(step == 0)
        def _():
            for i in range(4):
                weight[:, :, lax.rem(meta[50] + 4 - i, 4)] = parts[i][...]

    def body(x_ref):
        if store is store_keys:
            result = jnp.dot(
                x_ref[...],
                weight[...].reshape(DEPTH, 512),
                preferred_element_type=F32,
            )
        else:
            result = jnp.zeros((x_ref.shape[0], 512), F32)
            for i in range(4):
                start = pl.multiple_of(lax.rem(meta[49] + 4 - i, 4) * 512, 512)
                result += jnp.dot(
                    x_ref[:, pl.ds(start, 512)],
                    parts[i][...].reshape(512, 512),
                    preferred_element_type=F32,
                )
        store(result, turned, *out_refs)

    @pl.when(step == 0)
    def _():
        body(x_refs[0])

    @pl.when(step == 1)
    def _():
        body(x_refs[1])


def store_queries(result, turned, q_ref):
    for head in range(4):
        lanes = slice(128 * head, 128 * head + 128)
        q_ref[:, lanes] = turned(result[:, lanes])


def store_keys(result, turned, kvt_ref, v_ref):
    for head in range(2):
        kvt_ref[head] = turned(result[:, 128 * head : 128 * head + 128])
        value = result[:, 256 + 128 * head : 384 + 128 * head]
        v_ref[head] = value.astype(BF)
        for page in range(result.shape[0] // PAGE):
            rows = slice(PAGE * page, PAGE * page + PAGE)
            kvt_ref[2 + head, rows, :] = jnp.transpose(value[rows]).astype(BF)


def project(meta, sides, parts, tables, pair, kind):
    tile = TOK

    def table(i, m):
        return (jnp.bitwise_xor(m[0], 2 * i + pair), 0)

    if kind == "q":
        store = store_queries
        scratch = []
        out_specs = [pl.BlockSpec((tile, 512), lambda i, m: (i, 0))]
        out_shape = [jax.ShapeDtypeStruct((2 * TOK, 512), BF)]
    else:
        store = store_keys
        scratch = [pltpu.VMEM((4, 2, 4, 64, 512), BF)]
        out_specs = [
            pl.BlockSpec((4, tile, 128), lambda i, m: (0, i, 0)),
            pl.BlockSpec((2, tile, 128), lambda i, m: (0, i, 0)),
        ]
        out_shape = [
            jax.ShapeDtypeStruct((4, 2 * TOK, 128), BF),
            jax.ShapeDtypeStruct((2, 2 * TOK, 128), BF),
        ]
    return pl.pallas_call(
        functools.partial(project_kernel, store),
        grid_spec=pltpu.PrefetchScalarGridSpec(
            num_scalar_prefetch=1,
            grid=(2,),
            in_specs=[pl.BlockSpec((tile, DEPTH), lambda i, m: (0, 0))] * 2
            + [INSIDE] * 4
            + [pl.BlockSpec((tile, 128), table)] * 2,
            out_specs=out_specs,
            scratch_shapes=scratch,
        ),
        out_shape=out_shape,
        compiler_params=pltpu.CompilerParams(vmem_limit_bytes=40 << 20),
        cost_estimate=pl.CostEstimate(
            flops=4 * TOK * DEPTH * 512, transcendentals=0, bytes_accessed=8 << 20
        ),
    )(meta, *sides, *parts, *tables)


def attend_kernel(pair, meta, *refs):
    q_ref, own, halo, out_ref, kvt, saved, bias = (
        refs[0], refs[1:3], refs[3:5], *refs[5:]
    )
    role = meta[0]
    for p in range(4):
        block = jnp.bitwise_xor(role, 2 * (p % 2) + p // 2)
        source = slice((p % 2) * TOK, (p % 2) * TOK + TOK)
        for at, side in ((0, halo), (4, own)):
            rows = pl.ds(pl.multiple_of((block + at) * TOK, TOK), TOK)
            kvt[:, rows, :] = side[p // 2][:, source, :]
    kvt[:, pl.ds(2 * QTOK, CHUNK), :] = jnp.zeros((4, CHUNK, 128), BF)
    gap = lax.broadcasted_iota(jnp.int32, (CHUNK, 256), 0) - (
        lax.broadcasted_iota(jnp.int32, (CHUNK, 256), 1) % PAGE
    )
    for i in range(2):
        bias[i] = jnp.where(gap <= i * PAGE, 0.0, NEG)
    factor = (1.0 / math.sqrt(128)) * math.log2(math.e)
    tall = lax.broadcasted_iota(jnp.int32, (PAGE, 128), 0)

    def one_page(index, carry):
        rows = pl.ds(pl.multiple_of(index * PAGE, PAGE), PAGE)
        page = jnp.bitwise_xor(role, 2 * (index // 4) + pair) * 4 + index % 4
        offset = meta[1 + page]
        live = meta[17 + page]
        low = QPAGES + page - offset
        full = offset // 2
        stack = [
            jnp.concatenate(
                [
                    q_ref[rows, 256 * h : 256 * h + 128],
                    q_ref[rows, 256 * h + 128 : 256 * h + 256],
                ],
                axis=0,
            )
            for h in range(2)
        ]

        def scan(chunk, tops, count, masked):
            base = pl.multiple_of((low + 2 * chunk) * PAGE, PAGE)
            result = []
            for h in range(2):
                scores = lax.dot_general(
                    kvt[h, pl.ds(base, count * CHUNK), :],
                    stack[h],
                    (((1,), (1,)), ((), ())),
                    preferred_element_type=F32,
                )
                if masked:
                    scores = scores + bias[offset % 2]
                for i in range(count):
                    saved[h, chunk + i] = scores[CHUNK * i : CHUNK * i + CHUNK]
                peak = jnp.max(scores.reshape(count * CHUNK // 8, 8, 256), axis=0)
                result.append(jnp.maximum(tops[h], peak))
            return tuple(result)

        tops = (jnp.full((8, 256), NEG, F32),) * 2
        tops = lax.fori_loop(
            0, full // 2, lambda i, t: scan(2 * i, t, 2, False), tops
        )
        tops = lax.fori_loop(
            full // 2 * 2, full, lambda i, t: scan(i, t, 1, False), tops
        )
        tops = scan(full, tops, 1, True)
        tops = [jnp.max(top, axis=0, keepdims=True) for top in tops]

        def fold(chunk, state, count):
            result = []
            for h in range(2):
                total, acc = state[h]
                parts, weights = [], []
                for i in range(count):
                    expo = jnp.exp2((saved[h, chunk + i] - tops[h]) * factor)
                    total = total + jnp.sum(expo.reshape(CHUNK // 8, 8, 256), axis=0)
                    weights.append(expo.astype(BF))
                for i in range(2 * count):
                    at = pl.multiple_of((low + 2 * chunk + i) * PAGE, PAGE)
                    parts.append(kvt[2 + h, pl.ds(at, PAGE), :])
                acc = acc + jnp.dot(
                    jnp.concatenate(parts, axis=1),
                    jnp.concatenate(weights, axis=0),
                    preferred_element_type=F32,
                )
                result.append((total, acc))
            return tuple(result)

        state = ((jnp.zeros((8, 256), F32), jnp.zeros((128, 256), F32)),) * 2
        count = full + 1
        state = lax.fori_loop(0, count // 2, lambda i, s: fold(2 * i, s, 2), state)
        state = lax.fori_loop(
            count // 2 * 2, count, lambda i, s: fold(i, s, 1), state
        )
        for h in range(2):
            total, acc = state[h]
            value = acc / jnp.sum(total, axis=0, keepdims=True)
            value = jnp.transpose(value)
            for g in range(2):
                part = value[128 * g : 128 * g + 128]
                part = jnp.where(tall < live, part, 0.0)
                at_lane = 256 * h + 128 * g
                out_ref[rows, at_lane : at_lane + 128] = part.astype(BF)
        return carry

    lax.fori_loop(0, 8, one_page, 0)


def attend(meta, queries, own, halo, pair):
    return pl.pallas_call(
        functools.partial(attend_kernel, pair),
        grid_spec=pltpu.PrefetchScalarGridSpec(
            num_scalar_prefetch=1,
            grid=(),
            in_specs=[INSIDE] * 5,
            out_specs=INSIDE,
            scratch_shapes=[
                pltpu.VMEM((4, 2 * QTOK + CHUNK, 128), BF),
                pltpu.VMEM((2, 9, CHUNK, 256), F32),
                pltpu.VMEM((2, CHUNK, 256), F32),
            ],
        ),
        out_shape=jax.ShapeDtypeStruct((2 * TOK, 512), BF),
        compiler_params=pltpu.CompilerParams(vmem_limit_bytes=40 << 20),
        cost_estimate=pl.CostEstimate(
            flops=4 << 30, transcendentals=4 << 20, bytes_accessed=6 << 20
        ),
    )(meta, queries, *own, *halo)


def pack_kernel(meta, *refs):
    keys, values, out_refs, kv = refs[:2], refs[2:4], refs[4:8], refs[8]
    role = meta[0]
    for p in range(4):
        block = jnp.bitwise_xor(role, 2 * (p % 2) + p // 2)
        rows = pl.ds(pl.multiple_of(block * TOK, TOK), TOK)
        source = slice((p % 2) * TOK, (p % 2) * TOK + TOK)
        kv[:2, rows, :] = keys[p // 2][:2, source, :]
        kv[2:, rows, :] = values[p // 2][:, source, :]
    tall = lax.broadcasted_iota(jnp.int32, (PAGE, 128), 0)
    for p in range(4):
        target = jnp.bitwise_xor(role, p)
        for slot in range(4):
            page = meta[33 + target * 4 + slot]
            live = meta[17 + page]
            rows = pl.ds(pl.multiple_of(page * PAGE, PAGE), PAGE)
            for part in range(4):
                block = jnp.where(tall < live, kv[part, rows, :].astype(F32), 0.0)
                lanes = slice(128 * part, 128 * part + 128)
                out_refs[p][PAGE * slot : PAGE * slot + PAGE, lanes] = block.astype(BF)


def pack(meta, keys, values):
    return pl.pallas_call(
        pack_kernel,
        grid_spec=pltpu.PrefetchScalarGridSpec(
            num_scalar_prefetch=1,
            grid=(),
            in_specs=[INSIDE] * 4,
            out_specs=[INSIDE] * 4,
            scratch_shapes=[pltpu.VMEM((4, QTOK, 128), BF)],
        ),
        out_shape=[jax.ShapeDtypeStruct((TOK, 512), BF)] * 4,
        compiler_params=pltpu.CompilerParams(vmem_limit_bytes=30 << 20),
        name="pack_pages",
    )(meta, *keys, *values)


def unpack_kernel(meta, *refs):
    in_refs, key_ref, value_ref = refs[:4], refs[4], refs[5]
    step = pl.program_id(0)
    for p in range(4):

        @pl.when(step == p)
        def _(p=p):
            key_ref[...] = in_refs[p][:, :256]
            value_ref[...] = in_refs[p][:, 256:]


def unpack(meta, received):
    whole = pl.BlockSpec((TOK, 512), lambda i, m: (0, 0))
    column = pl.BlockSpec((TOK, 256), lambda i, m: (0, jnp.bitwise_xor(m[0], i)))
    return pl.pallas_call(
        unpack_kernel,
        grid_spec=pltpu.PrefetchScalarGridSpec(
            num_scalar_prefetch=1,
            grid=(4,),
            in_specs=[whole] * 4,
            out_specs=[column] * 2,
        ),
        out_shape=[jax.ShapeDtypeStruct((TOK, 1024), BF)] * 2,
        compiler_params=pltpu.CompilerParams(vmem_limit_bytes=30 << 20),
        name="unpack_pages",
    )(meta, *received)


def fill_rows(meta, parts, weight, parity):
    for half in range(2):
        for d in range(4):
            flip = jnp.bitwise_xor(lax.rem(meta[49] + d, 4), meta[0])

            @pl.when(lax.rem(flip, 2) == parity)
            def _(half=half, d=d, flip=flip):
                weight[half, flip // 2] = parts[4 * half + d][...].reshape(512, 1024)


def pair_product(in_refs, weight, half):
    return jnp.dot(
        in_refs[0][:TOK], weight[half, 0], preferred_element_type=F32
    ) + jnp.dot(in_refs[1][...], weight[half, 1], preferred_element_type=F32)


def near_kernel(meta, *refs):
    in_refs, parts, out_ref, weight = refs[:2], refs[2:10], refs[10], refs[11]
    fill_rows(meta, parts, weight, 0)
    for half in range(2):
        out_ref[half] = pair_product(in_refs, weight, half)


def far_kernel(meta, *refs):
    in_refs, parts, partial, out_ref, weight = (
        refs[:2], refs[2:10], refs[10], refs[11], refs[12]
    )
    step = pl.program_id(0)

    @pl.when(step == 0)
    def _():
        fill_rows(meta, parts, weight, 1)

    for half in range(2):

        @pl.when(step == half)
        def _(half=half):
            total = partial[half] + pair_product(in_refs, weight, half)
            out_ref[...] = total.astype(BF)


def output_near(meta, pair, parts):
    return pl.pallas_call(
        near_kernel,
        grid_spec=pltpu.PrefetchScalarGridSpec(
            num_scalar_prefetch=1,
            grid=(),
            in_specs=[INSIDE] * 10,
            out_specs=INSIDE,
            scratch_shapes=[pltpu.VMEM((2, 2, 512, 1024), BF)],
        ),
        out_shape=jax.ShapeDtypeStruct((2, TOK, 1024), F32),
        compiler_params=pltpu.CompilerParams(vmem_limit_bytes=32 << 20),
        name="output_near",
    )(meta, *pair, *parts)


def output_far(meta, pair, parts, partial):
    return pl.pallas_call(
        far_kernel,
        grid_spec=pltpu.PrefetchScalarGridSpec(
            num_scalar_prefetch=1,
            grid=(2,),
            in_specs=[INSIDE] * 11,
            out_specs=pl.BlockSpec(
                (TOK, 1024), lambda i, m: (0, jnp.bitwise_xor(m[0] // 2, i))
            ),
            scratch_shapes=[pltpu.VMEM((2, 2, 512, 1024), BF)],
        ),
        out_shape=jax.ShapeDtypeStruct((TOK, DEPTH), BF),
        compiler_params=pltpu.CompilerParams(vmem_limit_bytes=32 << 20),
        name="output_far",
    )(meta, *pair, *parts, partial)


def page_sources(page_slots, core):
    other = swap(page_slots, "c")
    first = jnp.where(core == 0, page_slots, other)
    second = jnp.where(core == 0, other, page_slots)
    slots = jnp.stack([first, second])
    wanted = jnp.arange(8, dtype=jnp.int32)
    hit = slots[:, None, :] == wanted[None, :, None]
    found = jnp.sum(jnp.where(hit, wanted[None, None, :], 0), axis=2)
    return (found + jnp.array([[0], [8]], jnp.int32)).reshape(16)


def previous_quad(block):
    names = ("y", "zl", "x", "c", "zh")
    route = [(i, i + 4) for i in range(124)]
    return lax.ppermute(block, names, route)


def shards(hidden_in, norm_gain, w_qk, w_v, w_o, prompt_pages, last_fill, page_slots):
    core = lax.axis_index("c")
    role = core * 2 + lax.axis_index("zh")
    y, x = lax.axis_index("y"), lax.axis_index("x")
    quad = (y * 2 + lax.axis_index("zl")) * 4 + x

    here = jnp.stack([role, y, x]).astype(jnp.int32)

    slices = small(slices_kernel, here, (w_qk, w_v, w_o), [(8, 16, 2048)])[0]
    level = lax.all_to_all(
        slices, ("zl", "c", "zh"), split_axis=0, concat_axis=0, tiled=True
    ).reshape(2, 64, 2048)
    kv_level, q_level, o_level = small(
        split_kernel, here, (level,), [(2, 64, 512), (2, 64, 512), (2, 64, 1024)]
    )
    kv_row = small(
        column_kernel, here, ring_pieces(kv_level, "y"), [(4, 2, 64, 512)]
    )[0]
    kv_parts = ring_pieces(kv_row, "x")
    q_row = small(arrange_kernel, here, ring_pieces(q_level, "x"), [(2, 4, 64, 512)])[0]
    q_parts = ring_pieces(q_row, "y")
    o_row = small(
        arrange_kernel, here, ring_pieces(o_level, "x"), [(2, 4, 64, 1024)]
    )[0]
    o_parts = ring_chain(o_row, "y")

    normed = normalize(after(hidden_in, slices), norm_gain)
    beside = swap(normed, "c")
    across = swap(after(normed, level), "zh")
    diagonal = swap(across, "c")

    offset, live = page_tables(prompt_pages, last_fill, quad * QPAGES)
    sources = page_sources(page_slots, core)
    meta = jnp.concatenate(
        [role[None], offset, live, sources, y[None], x[None]]
    ).astype(jnp.int32)
    tables = rotation_tables(offset)

    sides = ((normed, beside), (across, diagonal))
    keys, values, halo, queries = [], [], [], []
    metas = (meta, tick(meta))
    for pair in range(2):
        kvt, v = project(metas[pair], sides[pair], kv_parts, tables, pair, "kv")
        keys.append(kvt)
        values.append(v)
        halo.append(previous_quad(kvt))
        queries += project(meta, sides[pair], q_parts, tables, pair, "q")
    packed = pack(meta, keys, values)
    pages = [packed[0]]
    for flip in (1, 2, 3):
        pages.append(to_role(packed[flip], flip))

    far = attend(meta, queries[1], keys, halo, 1)
    far = swap(far, "zh")
    near = attend(meta, queries[0], keys, halo, 0)
    o_parts = list(o_parts)
    for i in range(4):
        o_parts.append(swap(o_parts[i], "c"))
    partial = output_near(meta, (near, swap(near[TOK:], "c")), o_parts)
    diagonal_far = swap(far[TOK:], "c")
    attended = output_far(meta, (far, diagonal_far), o_parts, partial)
    key_cache, value_cache = unpack(meta, pages)
    return (
        attended,
        key_cache.reshape(4, PAGE, 1024),
        value_cache.reshape(4, PAGE, 1024),
    )


def solution(mesh):
    fine = Mesh(mesh.devices.reshape(SIZES), AXES)
    rows = P(AXES, None)
    in_specs = (rows, P(), rows, rows, rows, P(), P(), P(("y", "zl", "x", "c")))
    out_specs = (rows, P(AXES, None, None), P(AXES, None, None))
    return jax.shard_map(
        shards, mesh=fine, in_specs=in_specs, out_specs=out_specs, check_vma=False
    )
```

```python
import functools
import math

import jax
import jax.numpy as jnp
from jax import lax
from jax.experimental import pallas as pl
from jax.experimental.pallas import tpu as pltpu
from jax.sharding import Mesh, PartitionSpec as P


AXES = ("y", "zl", "x", "c", "zh")
SIZES = (4, 2, 4, 2, 2)
QUAD = ("c", "zh")
DEPTH = 2048
TOK = 512
PAGE = 128
QTOK = 4 * TOK
QPAGES = QTOK // PAGE
CHUNK = 256
THETA = 1000000.0
EPS = 1e-05
NEG = -1e30
BF = jnp.bfloat16
INSIDE = pl.BlockSpec(memory_space=pltpu.VMEM)
F32 = jnp.float32


def swap(block, axis):
    return lax.ppermute(block, axis, [(0, 1), (1, 0)])


def shift(block, axis, distance):
    return lax.ppermute(block, axis, [(i, (i + distance) % 4) for i in range(4)])


def to_role(block, flip):
    return lax.ppermute(block, QUAD, [(i, i ^ flip) for i in range(4)])


def ring_pieces(block, axis):
    pieces = [block]
    for distance in (1, 2, 3):
        pieces.append(shift(block, axis, distance))
    return pieces


def ring_chain(block, axis):
    pieces = [block]
    for _ in range(2):
        pieces.append(shift(pieces[-1], axis, -1))
    pieces.append(shift(block, axis, 1))
    return pieces


def slices_kernel(here, qk_ref, v_ref, o_ref, out_ref):
    for role in range(4):
        for copy in (role, role + 4):
            out_ref[copy, :, :512] = qk_ref[:, 512 * role : 512 * role + 512]
            first = 2048 + 256 * role
            out_ref[copy, :, 512:768] = qk_ref[:, first : first + 256]
            out_ref[copy, :, 768:1024] = v_ref[:, 256 * role : 256 * role + 256]
            first = 1024 * (role // 2)
            out_ref[copy, :, 1024:] = o_ref[:, first : first + 1024]


def split_kernel(here, level_ref, kv_ref, q_ref, o_ref):
    kv_ref[...] = level_ref[:, :, 512:1024]
    q_ref[...] = level_ref[:, :, :512]
    o_ref[...] = level_ref[:, :, 1024:]


def arrange_kernel(here, *refs):
    pieces, outs = refs[:4], refs[4:]
    for k in range(4):
        place = lax.rem(here[2] + 4 - k, 4)
        first = 0
        for out_ref in outs:
            width = out_ref.shape[3]
            out_ref[:, place] = pieces[k][:, :, first : first + width]
            first += width


def column_kernel(here, *refs):
    for k in range(4):
        refs[4][lax.rem(here[1] + 4 - k, 4)] = refs[k][...]


def tick_kernel(in_ref, out_ref):
    for i in range(51):
        out_ref[i] = in_ref[i]


def tick(meta):
    scalars = pl.BlockSpec(memory_space=pltpu.SMEM)
    return pl.pallas_call(
        tick_kernel,
        in_specs=[scalars],
        out_specs=scalars,
        out_shape=jax.ShapeDtypeStruct((51,), jnp.int32),
        name="tick",
    )(meta)


def small(kernel, here, operands, shapes):
    return pl.pallas_call(
        kernel,
        grid_spec=pltpu.PrefetchScalarGridSpec(
            num_scalar_prefetch=1,
            grid=(),
            in_specs=[INSIDE] * len(operands),
            out_specs=[INSIDE] * len(shapes),
        ),
        out_shape=[jax.ShapeDtypeStruct(shape, BF) for shape in shapes],
        compiler_params=pltpu.CompilerParams(vmem_limit_bytes=20 << 20),
    )(here, *operands)


def after(block, *others):
    return lax.optimization_barrier((block, *others))[0]


def normalize(hidden_in, norm_gain):
    values = hidden_in.astype(F32)
    scale = lax.rsqrt(jnp.mean(values * values, axis=-1, keepdims=True) + EPS)
    return (values * scale * norm_gain[None, :]).astype(BF)


def page_tables(prompt_pages, last_fill, first_page):
    count = prompt_pages.shape[0]
    order = jnp.arange(count, dtype=jnp.int32)
    ends = jnp.sum(
        jnp.where(order[None, :] <= order[:, None], prompt_pages[None, :], 0), axis=1
    )
    pages = first_page + jnp.arange(QPAGES, dtype=jnp.int32)
    before = ends[None, :] <= pages[:, None]
    start = jnp.max(jnp.where(before, ends[None, :], 0), axis=1)
    closing = ends[None, :] == pages[:, None] + 1
    short = jnp.sum(jnp.where(closing, PAGE - last_fill[None, :], 0), axis=1)
    return pages - start, PAGE - short


def rotation_tables(offset):
    row = jnp.arange(PAGE, dtype=jnp.int32)
    position = (offset[:, None] * PAGE + row[None, :]).reshape(QTOK)
    half = 64
    freq = jnp.power(THETA, -2.0 * jnp.arange(half, dtype=F32) / 128)
    angle = position.astype(F32)[:, None] * freq[None, :]
    cosine, sine = jnp.cos(angle), jnp.sin(angle)
    return (
        jnp.concatenate([cosine, cosine], axis=-1),
        jnp.concatenate([-sine, sine], axis=-1),
    )


def project_kernel(store, meta, *refs):
    x_refs, parts, tables, out_refs = refs[:2], refs[2:6], refs[6:8], refs[8:]
    if store is store_keys:
        out_refs, weight = out_refs[:-1], out_refs[-1]
    step = pl.program_id(0)
    cosine = tables[0][...]
    sine = tables[1][...]

    def turned(block):
        return (block * cosine + pltpu.roll(block, 64, 1) * sine).astype(BF)

    if store is store_keys:

        @pl.when(step == 0)
        def _():
            for i in range(4):
                weight[:, :, lax.rem(meta[50] + 4 - i, 4)] = parts[i][...]

    def body(x_ref):
        if store is store_keys:
            result = jnp.dot(
                x_ref[...],
                weight[...].reshape(DEPTH, 512),
                preferred_element_type=F32,
            )
        else:
            result = jnp.zeros((x_ref.shape[0], 512), F32)
            for i in range(4):
                start = pl.multiple_of(lax.rem(meta[49] + 4 - i, 4) * 512, 512)
                result += jnp.dot(
                    x_ref[:, pl.ds(start, 512)],
                    parts[i][...].reshape(512, 512),
                    preferred_element_type=F32,
                )
        store(result, turned, *out_refs)

    @pl.when(step == 0)
    def _():
        body(x_refs[0])

    @pl.when(step == 1)
    def _():
        body(x_refs[1])


def store_queries(result, turned, q_ref):
    for head in range(4):
        lanes = slice(128 * head, 128 * head + 128)
        q_ref[:, lanes] = turned(result[:, lanes])


def store_keys(result, turned, kvt_ref, v_ref):
    for head in range(2):
        kvt_ref[head] = turned(result[:, 128 * head : 128 * head + 128])
        value = result[:, 256 + 128 * head : 384 + 128 * head]
        v_ref[head] = value.astype(BF)
        for page in range(result.shape[0] // PAGE):
            rows = slice(PAGE * page, PAGE * page + PAGE)
            kvt_ref[2 + head, rows, :] = jnp.transpose(value[rows]).astype(BF)


def project(meta, sides, parts, tables, pair, kind):
    tile = TOK

    def table(i, m):
        return (jnp.bitwise_xor(m[0], 2 * i + pair), 0)

    if kind == "q":
        store = store_queries
        scratch = []
        out_specs = [pl.BlockSpec((tile, 512), lambda i, m: (i, 0))]
        out_shape = [jax.ShapeDtypeStruct((2 * TOK, 512), BF)]
    else:
        store = store_keys
        scratch = [pltpu.VMEM((4, 2, 4, 64, 512), BF)]
        out_specs = [
            pl.BlockSpec((4, tile, 128), lambda i, m: (0, i, 0)),
            pl.BlockSpec((2, tile, 128), lambda i, m: (0, i, 0)),
        ]
        out_shape = [
            jax.ShapeDtypeStruct((4, 2 * TOK, 128), BF),
            jax.ShapeDtypeStruct((2, 2 * TOK, 128), BF),
        ]
    return pl.pallas_call(
        functools.partial(project_kernel, store),
        grid_spec=pltpu.PrefetchScalarGridSpec(
            num_scalar_prefetch=1,
            grid=(2,),
            in_specs=[pl.BlockSpec((tile, DEPTH), lambda i, m: (0, 0))] * 2
            + [INSIDE] * 4
            + [pl.BlockSpec((tile, 128), table)] * 2,
            out_specs=out_specs,
            scratch_shapes=scratch,
        ),
        out_shape=out_shape,
        compiler_params=pltpu.CompilerParams(vmem_limit_bytes=40 << 20),
        cost_estimate=pl.CostEstimate(
            flops=4 * TOK * DEPTH * 512, transcendentals=0, bytes_accessed=8 << 20
        ),
    )(meta, *sides, *parts, *tables)


def attend_pages(pair, mode, meta, q_ref, out_ref, kvt, saved, bias, parts):
    role = meta[0]
    factor = (1.0 / math.sqrt(128)) * math.log2(math.e)
    tall = lax.broadcasted_iota(jnp.int32, (PAGE, 128), 0)

    def one_page(index, carry):
        rows = pl.ds(pl.multiple_of(index * PAGE, PAGE), PAGE)
        page = jnp.bitwise_xor(role, 2 * (index // 4) + pair) * 4 + index % 4
        live = meta[17 + page]
        reach = meta[1 + page]
        stack = [
            jnp.concatenate(
                [
                    q_ref[rows, 256 * h : 256 * h + 128],
                    q_ref[rows, 256 * h + 128 : 256 * h + 256],
                ],
                axis=0,
            )
            for h in range(2)
        ]

        def run(first, opened, closed, covered, shade, count):
            def scan(chunk, tops, width, masked):
                base = pl.multiple_of((first + 2 * chunk) * PAGE, PAGE)
                result = []
                for h in range(2):
                    scores = lax.dot_general(
                        kvt[h, pl.ds(base, width * CHUNK), :],
                        stack[h],
                        (((1,), (1,)), ((), ())),
                        preferred_element_type=F32,
                    )
                    if masked:
                        scores = scores + bias[shade]
                    for i in range(width):
                        saved[h, chunk + i] = scores[CHUNK * i : CHUNK * i + CHUNK]
                    peak = jnp.max(scores.reshape(width * CHUNK // 8, 8, 256), axis=0)
                    result.append(jnp.maximum(tops[h], peak))
                return tuple(result)

            tops = (jnp.full((8, 256), NEG, F32),) * 2
            twice = (closed - opened) // 2
            tops = lax.fori_loop(
                0, twice, lambda i, t: scan(opened + 2 * i, t, 2, False), tops
            )
            tops = lax.fori_loop(
                opened + 2 * twice, closed, lambda i, t: scan(i, t, 1, False), tops
            )
            tops = scan(covered, tops, 1, True)
            tops = [jnp.max(top, axis=0, keepdims=True) for top in tops]

            def fold(chunk, state, width):
                result = []
                for h in range(2):
                    total, acc = state[h]
                    pieces, weights = [], []
                    for i in range(width):
                        expo = jnp.exp2((saved[h, chunk + i] - tops[h]) * factor)
                        total = total + jnp.sum(
                            expo.reshape(CHUNK // 8, 8, 256), axis=0
                        )
                        weights.append(expo.astype(BF))
                    for i in range(2 * width):
                        at = pl.multiple_of((first + 2 * chunk + i) * PAGE, PAGE)
                        pieces.append(kvt[2 + h, pl.ds(at, PAGE), :])
                    acc = acc + jnp.dot(
                        jnp.concatenate(pieces, axis=1),
                        jnp.concatenate(weights, axis=0),
                        preferred_element_type=F32,
                    )
                    result.append((total, acc))
                return tuple(result)

            state = ((jnp.zeros((8, 256), F32), jnp.zeros((128, 256), F32)),) * 2
            state = lax.fori_loop(0, count // 2, lambda i, s: fold(2 * i, s, 2), state)
            state = lax.fori_loop(
                count // 2 * 2, count, lambda i, s: fold(i, s, 1), state
            )
            return [
                (tops[h], jnp.sum(state[h][0], axis=0, keepdims=True), state[h][1])
                for h in range(2)
            ]

        def finish(h, total, acc):
            value = jnp.transpose(acc / total)
            for g in range(2):
                part = value[128 * g : 128 * g + 128]
                part = jnp.where(tall < live, part, 0.0)
                at_lane = 256 * h + 128 * g
                out_ref[rows, at_lane : at_lane + 128] = part.astype(BF)

        if mode == "halo":
            pages = jnp.maximum(reach - page, 0)
            count = (pages + 1) // 2
            peaks, totals, sums = parts

            @pl.when(count > 0)
            def _():
                result = run(QPAGES - 2 * count, 1, count, 0, 2 + pages % 2, count)
                for h in range(2):
                    top, total, acc = result[h]
                    before = peaks[index, h][:1]
                    higher = jnp.maximum(top, before)
                    fade = jnp.exp2((top - higher) * factor)
                    keep = jnp.exp2((before - higher) * factor)
                    total = total * fade + totals[index, h][:1] * keep
                    acc = acc * fade + sums[index, h] * keep
                    finish(h, total, acc)

            @pl.when(count == 0)
            def _():
                for h in range(2):
                    finish(h, totals[index, h][:1], sums[index, h])

            return carry

        offset = jnp.minimum(reach, page) if mode == "own" else reach
        full = offset // 2
        result = run(QPAGES + page - offset, 0, full, full, offset % 2, full + 1)
        for h in range(2):
            top, total, acc = result[h]
            if mode == "own":
                peaks, totals, sums = parts
                peaks[index, h] = jnp.broadcast_to(top, (8, 256))
                totals[index, h] = jnp.broadcast_to(total, (8, 256))
                sums[index, h] = acc
            else:
                finish(h, total, acc)
        return carry

    lax.fori_loop(0, 8, one_page, 0)


def fill_pages(role, sides, kvt):
    for p in range(4):
        block = jnp.bitwise_xor(role, 2 * (p % 2) + p // 2)
        source = slice((p % 2) * TOK, (p % 2) * TOK + TOK)
        for at, side in sides:
            rows = pl.ds(pl.multiple_of((block + at) * TOK, TOK), TOK)
            kvt[:, rows, :] = side[p // 2][:, source, :]


def fill_bias(bias):
    key = lax.broadcasted_iota(jnp.int32, (CHUNK, 256), 0)
    gap = key - lax.broadcasted_iota(jnp.int32, (CHUNK, 256), 1) % PAGE
    for i in range(2):
        bias[i] = jnp.where(gap <= i * PAGE, 0.0, NEG)
    bias[2] = jnp.zeros((CHUNK, 256), F32)
    bias[3] = jnp.where(key < PAGE, NEG, 0.0)


def whole_kernel(pair, meta, q_ref, own0, own1, halo0, halo1, out_ref, kvt, saved, bias):
    fill_pages(meta[0], ((0, (halo0, halo1)), (4, (own0, own1))), kvt)
    kvt[:, pl.ds(2 * QTOK, CHUNK), :] = jnp.zeros((4, CHUNK, 128), BF)
    fill_bias(bias)
    attend_pages(pair, "all", meta, q_ref, out_ref, kvt, saved, bias, None)


def own_kernel(pair, meta, q_ref, own0, own1, peaks, totals, sums, kvt, saved, bias):
    fill_pages(meta[0], ((4, (own0, own1)),), kvt)
    kvt[:, pl.ds(2 * QTOK, CHUNK), :] = jnp.zeros((4, CHUNK, 128), BF)
    fill_bias(bias)
    parts = (peaks, totals, sums)
    attend_pages(pair, "own", meta, q_ref, None, kvt, saved, bias, parts)


def halo_kernel(pair, meta, q_ref, halo0, halo1, peaks, totals, sums, out_ref, *scratch):
    kvt, saved, bias = scratch
    fill_pages(meta[0], ((0, (halo0, halo1)),), kvt)
    fill_bias(bias)
    parts = (peaks, totals, sums)
    attend_pages(pair, "halo", meta, q_ref, out_ref, kvt, saved, bias, parts)


def attend_call(kernel, pair, meta, operands, shapes):
    return pl.pallas_call(
        functools.partial(kernel, pair),
        grid_spec=pltpu.PrefetchScalarGridSpec(
            num_scalar_prefetch=1,
            grid=(),
            in_specs=[INSIDE] * len(operands),
            out_specs=[INSIDE] * len(shapes),
            scratch_shapes=[
                pltpu.VMEM((4, 2 * QTOK + CHUNK, 128), BF),
                pltpu.VMEM((2, 9, CHUNK, 256), F32),
                pltpu.VMEM((4, CHUNK, 256), F32),
            ],
        ),
        out_shape=shapes,
        compiler_params=pltpu.CompilerParams(vmem_limit_bytes=40 << 20),
        cost_estimate=pl.CostEstimate(
            flops=2 << 30, transcendentals=2 << 20, bytes_accessed=6 << 20
        ),
    )(meta, *operands)


ROWS = [jax.ShapeDtypeStruct((2 * TOK, 512), BF)]
STATE = [
    jax.ShapeDtypeStruct((8, 2, 8, 256), F32),
    jax.ShapeDtypeStruct((8, 2, 8, 256), F32),
    jax.ShapeDtypeStruct((8, 2, 128, 256), F32),
]


def attend(meta, queries, own, halo, pair):
    operands = (queries, *own, *halo)
    return attend_call(whole_kernel, pair, meta, operands, ROWS)[0]


def attend_own(meta, queries, own, pair):
    return attend_call(own_kernel, pair, meta, (queries, *own), STATE)


def attend_halo(meta, queries, halo, parts, pair):
    operands = (queries, *halo, *parts)
    return attend_call(halo_kernel, pair, meta, operands, ROWS)[0]


def pack_kernel(meta, *refs):
    keys, values, out_refs, kv = refs[:2], refs[2:4], refs[4:8], refs[8]
    role = meta[0]
    for p in range(4):
        block = jnp.bitwise_xor(role, 2 * (p % 2) + p // 2)
        rows = pl.ds(pl.multiple_of(block * TOK, TOK), TOK)
        source = slice((p % 2) * TOK, (p % 2) * TOK + TOK)
        kv[:2, rows, :] = keys[p // 2][:2, source, :]
        kv[2:, rows, :] = values[p // 2][:, source, :]
    tall = lax.broadcasted_iota(jnp.int32, (PAGE, 128), 0)
    for p in range(4):
        target = jnp.bitwise_xor(role, p)
        for slot in range(4):
            page = meta[33 + target * 4 + slot]
            live = meta[17 + page]
            rows = pl.ds(pl.multiple_of(page * PAGE, PAGE), PAGE)
            for part in range(4):
                block = jnp.where(tall < live, kv[part, rows, :].astype(F32), 0.0)
                lanes = slice(128 * part, 128 * part + 128)
                out_refs[p][PAGE * slot : PAGE * slot + PAGE, lanes] = block.astype(BF)


def pack(meta, keys, values):
    return pl.pallas_call(
        pack_kernel,
        grid_spec=pltpu.PrefetchScalarGridSpec(
            num_scalar_prefetch=1,
            grid=(),
            in_specs=[INSIDE] * 4,
            out_specs=[INSIDE] * 4,
            scratch_shapes=[pltpu.VMEM((4, QTOK, 128), BF)],
        ),
        out_shape=[jax.ShapeDtypeStruct((TOK, 512), BF)] * 4,
        compiler_params=pltpu.CompilerParams(vmem_limit_bytes=30 << 20),
        name="pack_pages",
    )(meta, *keys, *values)


def unpack_kernel(meta, *refs):
    in_refs, key_ref, value_ref = refs[:4], refs[4], refs[5]
    step = pl.program_id(0)
    for p in range(4):

        @pl.when(step == p)
        def _(p=p):
            key_ref[...] = in_refs[p][:, :256]
            value_ref[...] = in_refs[p][:, 256:]


def unpack(meta, received):
    whole = pl.BlockSpec((TOK, 512), lambda i, m: (0, 0))
    column = pl.BlockSpec((TOK, 256), lambda i, m: (0, jnp.bitwise_xor(m[0], i)))
    return pl.pallas_call(
        unpack_kernel,
        grid_spec=pltpu.PrefetchScalarGridSpec(
            num_scalar_prefetch=1,
            grid=(4,),
            in_specs=[whole] * 4,
            out_specs=[column] * 2,
        ),
        out_shape=[jax.ShapeDtypeStruct((TOK, 1024), BF)] * 2,
        compiler_params=pltpu.CompilerParams(vmem_limit_bytes=30 << 20),
        name="unpack_pages",
    )(meta, *received)


def fill_rows(meta, parts, weight, parity):
    for half in range(2):
        for d in range(4):
            flip = jnp.bitwise_xor(lax.rem(meta[49] + d, 4), meta[0])

            @pl.when(lax.rem(flip, 2) == parity)
            def _(half=half, d=d, flip=flip):
                weight[half, flip // 2] = parts[4 * half + d][...].reshape(512, 1024)


def pair_product(in_refs, weight, half):
    return jnp.dot(
        in_refs[0][:TOK], weight[half, 0], preferred_element_type=F32
    ) + jnp.dot(in_refs[1][...], weight[half, 1], preferred_element_type=F32)


def near_kernel(meta, *refs):
    in_refs, parts, out_ref, weight = refs[:2], refs[2:10], refs[10], refs[11]
    fill_rows(meta, parts, weight, 0)
    for half in range(2):
        out_ref[half] = pair_product(in_refs, weight, half)


def far_kernel(meta, *refs):
    in_refs, parts, partial, out_ref, weight = (
        refs[:2], refs[2:10], refs[10], refs[11], refs[12]
    )
    step = pl.program_id(0)

    @pl.when(step == 0)
    def _():
        fill_rows(meta, parts, weight, 1)

    for half in range(2):

        @pl.when(step == half)
        def _(half=half):
            total = partial[half] + pair_product(in_refs, weight, half)
            out_ref[...] = total.astype(BF)


def output_near(meta, pair, parts):
    return pl.pallas_call(
        near_kernel,
        grid_spec=pltpu.PrefetchScalarGridSpec(
            num_scalar_prefetch=1,
            grid=(),
            in_specs=[INSIDE] * 10,
            out_specs=INSIDE,
            scratch_shapes=[pltpu.VMEM((2, 2, 512, 1024), BF)],
        ),
        out_shape=jax.ShapeDtypeStruct((2, TOK, 1024), F32),
        compiler_params=pltpu.CompilerParams(vmem_limit_bytes=32 << 20),
        name="output_near",
    )(meta, *pair, *parts)


def output_far(meta, pair, parts, partial):
    return pl.pallas_call(
        far_kernel,
        grid_spec=pltpu.PrefetchScalarGridSpec(
            num_scalar_prefetch=1,
            grid=(2,),
            in_specs=[INSIDE] * 11,
            out_specs=pl.BlockSpec(
                (TOK, 1024), lambda i, m: (0, jnp.bitwise_xor(m[0] // 2, i))
            ),
            scratch_shapes=[pltpu.VMEM((2, 2, 512, 1024), BF)],
        ),
        out_shape=jax.ShapeDtypeStruct((TOK, DEPTH), BF),
        compiler_params=pltpu.CompilerParams(vmem_limit_bytes=32 << 20),
        name="output_far",
    )(meta, *pair, *parts, partial)


def page_sources(page_slots, core):
    other = swap(page_slots, "c")
    first = jnp.where(core == 0, page_slots, other)
    second = jnp.where(core == 0, other, page_slots)
    slots = jnp.stack([first, second])
    wanted = jnp.arange(8, dtype=jnp.int32)
    hit = slots[:, None, :] == wanted[None, :, None]
    found = jnp.sum(jnp.where(hit, wanted[None, None, :], 0), axis=2)
    return (found + jnp.array([[0], [8]], jnp.int32)).reshape(16)


def previous_quad(block):
    names = ("y", "zl", "x", "c", "zh")
    route = [(i, i + 4) for i in range(124)]
    return lax.ppermute(block, names, route)


def shards(hidden_in, norm_gain, w_qk, w_v, w_o, prompt_pages, last_fill, page_slots):
    core = lax.axis_index("c")
    role = core * 2 + lax.axis_index("zh")
    y, x = lax.axis_index("y"), lax.axis_index("x")
    quad = (y * 2 + lax.axis_index("zl")) * 4 + x

    here = jnp.stack([role, y, x]).astype(jnp.int32)

    slices = small(slices_kernel, here, (w_qk, w_v, w_o), [(8, 16, 2048)])[0]
    level = lax.all_to_all(
        slices, ("zl", "c", "zh"), split_axis=0, concat_axis=0, tiled=True
    ).reshape(2, 64, 2048)
    kv_level, q_level, o_level = small(
        split_kernel, here, (level,), [(2, 64, 512), (2, 64, 512), (2, 64, 1024)]
    )
    kv_row = small(
        column_kernel, here, ring_pieces(kv_level, "y"), [(4, 2, 64, 512)]
    )[0]
    kv_parts = ring_pieces(kv_row, "x")
    q_row = small(arrange_kernel, here, ring_pieces(q_level, "x"), [(2, 4, 64, 512)])[0]
    q_parts = ring_pieces(q_row, "y")
    o_row = small(
        arrange_kernel, here, ring_pieces(o_level, "x"), [(2, 4, 64, 1024)]
    )[0]
    o_parts = ring_chain(o_row, "y")

    normed = normalize(after(hidden_in, slices), norm_gain)
    beside = swap(normed, "c")
    across = swap(after(normed, level), "zh")
    diagonal = swap(across, "c")

    offset, live = page_tables(prompt_pages, last_fill, quad * QPAGES)
    sources = page_sources(page_slots, core)
    meta = jnp.concatenate(
        [role[None], offset, live, sources, y[None], x[None]]
    ).astype(jnp.int32)
    tables = rotation_tables(offset)

    sides = ((normed, beside), (across, diagonal))
    keys, values, halo, queries = [], [], [], []
    metas = (meta, tick(meta))
    for pair in range(2):
        kvt, v = project(metas[pair], sides[pair], kv_parts, tables, pair, "kv")
        keys.append(kvt)
        values.append(v)
        halo.append(previous_quad(kvt))
        queries += project(meta, sides[pair], q_parts, tables, pair, "q")
    packed = pack(meta, keys, values)
    pages = [packed[0]]
    for flip in (1, 2, 3):
        pages.append(to_role(packed[flip], flip))

    parts = attend_own(meta, queries[1], keys, 1)
    far = attend_halo(meta, queries[1], halo, parts, 1)
    far = swap(far, "zh")
    near = attend(meta, queries[0], keys, halo, 0)
    o_parts = list(o_parts)
    for i in range(4):
        o_parts.append(swap(o_parts[i], "c"))
    partial = output_near(meta, (near, swap(near[TOK:], "c")), o_parts)
    diagonal_far = swap(far[TOK:], "c")
    attended = output_far(meta, (far, diagonal_far), o_parts, partial)
    key_cache, value_cache = unpack(meta, pages)
    return (
        attended,
        key_cache.reshape(4, PAGE, 1024),
        value_cache.reshape(4, PAGE, 1024),
    )


def solution(mesh):
    fine = Mesh(mesh.devices.reshape(SIZES), AXES)
    rows = P(AXES, None)
    in_specs = (rows, P(), rows, rows, rows, P(), P(), P(("y", "zl", "x", "c")))
    out_specs = (rows, P(AXES, None, None), P(AXES, None, None))
    return jax.shard_map(
        shards, mesh=fine, in_specs=in_specs, out_specs=out_specs, check_vma=False
    )
```

```python
import functools
import math

import jax
import jax.numpy as jnp
from jax import lax
from jax.experimental import pallas as pl
from jax.experimental.pallas import tpu as pltpu
from jax.sharding import Mesh, PartitionSpec as P


AXES = ("y", "zl", "x", "c", "zh")
SIZES = (4, 2, 4, 2, 2)
QUAD = ("c", "zh")
DEPTH = 2048
TOK = 512
PAGE = 128
QTOK = 4 * TOK
QPAGES = QTOK // PAGE
CHUNK = 256
THETA = 1000000.0
EPS = 1e-05
NEG = -1e30
BF = jnp.bfloat16
INSIDE = pl.BlockSpec(memory_space=pltpu.VMEM)
F32 = jnp.float32


def swap(block, axis):
    return lax.ppermute(block, axis, [(0, 1), (1, 0)])


def shift(block, axis, distance):
    return lax.ppermute(block, axis, [(i, (i + distance) % 4) for i in range(4)])


def to_role(block, flip):
    return lax.ppermute(block, QUAD, [(i, i ^ flip) for i in range(4)])


def ring_pieces(block, axis):
    pieces = [block]
    for distance in (1, 2, 3):
        pieces.append(shift(block, axis, distance))
    return pieces


def ring_chain(block, axis):
    pieces = [block]
    for _ in range(2):
        pieces.append(shift(pieces[-1], axis, -1))
    pieces.append(shift(block, axis, 1))
    return pieces


def slices_kernel(here, qk_ref, v_ref, o_ref, out_ref):
    for role in range(4):
        for copy in (role, role + 4):
            out_ref[copy, :, :512] = qk_ref[:, 512 * role : 512 * role + 512]
            first = 2048 + 256 * role
            out_ref[copy, :, 512:768] = qk_ref[:, first : first + 256]
            out_ref[copy, :, 768:1024] = v_ref[:, 256 * role : 256 * role + 256]
            first = 1024 * (role // 2)
            out_ref[copy, :, 1024:] = o_ref[:, first : first + 1024]


def split_kernel(here, level_ref, kv_ref, q_ref, o_ref):
    kv_ref[...] = level_ref[:, :, 512:1024]
    q_ref[...] = level_ref[:, :, :512]
    o_ref[...] = level_ref[:, :, 1024:]


def arrange_kernel(here, *refs):
    pieces, outs = refs[:4], refs[4:]
    for k in range(4):
        place = lax.rem(here[2] + 4 - k, 4)
        first = 0
        for out_ref in outs:
            width = out_ref.shape[3]
            out_ref[:, place] = pieces[k][:, :, first : first + width]
            first += width


def column_kernel(here, *refs):
    for k in range(4):
        refs[4][lax.rem(here[1] + 4 - k, 4)] = refs[k][...]


def tick_kernel(in_ref, out_ref):
    for i in range(51):
        out_ref[i] = in_ref[i]


def tick(meta):
    scalars = pl.BlockSpec(memory_space=pltpu.SMEM)
    return pl.pallas_call(
        tick_kernel,
        in_specs=[scalars],
        out_specs=scalars,
        out_shape=jax.ShapeDtypeStruct((51,), jnp.int32),
        name="tick",
    )(meta)


def small(kernel, here, operands, shapes):
    return pl.pallas_call(
        kernel,
        grid_spec=pltpu.PrefetchScalarGridSpec(
            num_scalar_prefetch=1,
            grid=(),
            in_specs=[INSIDE] * len(operands),
            out_specs=[INSIDE] * len(shapes),
        ),
        out_shape=[jax.ShapeDtypeStruct(shape, BF) for shape in shapes],
        compiler_params=pltpu.CompilerParams(vmem_limit_bytes=20 << 20),
    )(here, *operands)


def after(block, *others):
    return lax.optimization_barrier((block, *others))[0]


def normalize(hidden_in, norm_gain):
    values = hidden_in.astype(F32)
    scale = lax.rsqrt(jnp.mean(values * values, axis=-1, keepdims=True) + EPS)
    return (values * scale * norm_gain[None, :]).astype(BF)


def page_tables(prompt_pages, last_fill, first_page):
    count = prompt_pages.shape[0]
    order = jnp.arange(count, dtype=jnp.int32)
    ends = jnp.sum(
        jnp.where(order[None, :] <= order[:, None], prompt_pages[None, :], 0), axis=1
    )
    pages = first_page + jnp.arange(QPAGES, dtype=jnp.int32)
    before = ends[None, :] <= pages[:, None]
    start = jnp.max(jnp.where(before, ends[None, :], 0), axis=1)
    closing = ends[None, :] == pages[:, None] + 1
    short = jnp.sum(jnp.where(closing, PAGE - last_fill[None, :], 0), axis=1)
    return pages - start, PAGE - short


def rotation_tables(offset):
    row = jnp.arange(PAGE, dtype=jnp.int32)
    position = (offset[:, None] * PAGE + row[None, :]).reshape(QTOK)
    half = 64
    freq = jnp.power(THETA, -2.0 * jnp.arange(half, dtype=F32) / 128)
    angle = position.astype(F32)[:, None] * freq[None, :]
    cosine, sine = jnp.cos(angle), jnp.sin(angle)
    return (
        jnp.concatenate([cosine, cosine], axis=-1),
        jnp.concatenate([-sine, sine], axis=-1),
    )


def project_kernel(store, meta, *refs):
    x_refs, parts, tables, out_refs = refs[:2], refs[2:6], refs[6:8], refs[8:]
    if store is store_keys:
        out_refs, weight = out_refs[:-1], out_refs[-1]
    step = pl.program_id(0)
    cosine = tables[0][...]
    sine = tables[1][...]

    def turned(block):
        return (block * cosine + pltpu.roll(block, 64, 1) * sine).astype(BF)

    if store is store_keys:

        @pl.when(step == 0)
        def _():
            for i in range(4):
                weight[:, :, lax.rem(meta[50] + 4 - i, 4)] = parts[i][...]

    def body(x_ref):
        if store is store_keys:
            result = jnp.dot(
                x_ref[...],
                weight[...].reshape(DEPTH, 512),
                preferred_element_type=F32,
            )
        else:
            result = jnp.zeros((x_ref.shape[0], 512), F32)
            for i in range(4):
                start = pl.multiple_of(lax.rem(meta[49] + 4 - i, 4) * 512, 512)
                result += jnp.dot(
                    x_ref[:, pl.ds(start, 512)],
                    parts[i][...].reshape(512, 512),
                    preferred_element_type=F32,
                )
        store(result, turned, *out_refs)

    @pl.when(step == 0)
    def _():
        body(x_refs[0])

    @pl.when(step == 1)
    def _():
        body(x_refs[1])


def store_queries(result, turned, q_ref):
    for head in range(4):
        lanes = slice(128 * head, 128 * head + 128)
        q_ref[:, lanes] = turned(result[:, lanes])


def store_keys(result, turned, kvt_ref, v_ref):
    for head in range(2):
        kvt_ref[head] = turned(result[:, 128 * head : 128 * head + 128])
        value = result[:, 256 + 128 * head : 384 + 128 * head]
        v_ref[head] = value.astype(BF)
        for page in range(result.shape[0] // PAGE):
            rows = slice(PAGE * page, PAGE * page + PAGE)
            kvt_ref[2 + head, rows, :] = jnp.transpose(value[rows]).astype(BF)


def project(meta, sides, parts, tables, pair, kind):
    tile = TOK

    def table(i, m):
        return (jnp.bitwise_xor(m[0], 2 * i + pair), 0)

    if kind == "q":
        store = store_queries
        scratch = []
        out_specs = [pl.BlockSpec((tile, 512), lambda i, m: (i, 0))]
        out_shape = [jax.ShapeDtypeStruct((2 * TOK, 512), BF)]
    else:
        store = store_keys
        scratch = [pltpu.VMEM((4, 2, 4, 64, 512), BF)]
        out_specs = [
            pl.BlockSpec((4, tile, 128), lambda i, m: (0, i, 0)),
            pl.BlockSpec((2, tile, 128), lambda i, m: (0, i, 0)),
        ]
        out_shape = [
            jax.ShapeDtypeStruct((4, 2 * TOK, 128), BF),
            jax.ShapeDtypeStruct((2, 2 * TOK, 128), BF),
        ]
    return pl.pallas_call(
        functools.partial(project_kernel, store),
        grid_spec=pltpu.PrefetchScalarGridSpec(
            num_scalar_prefetch=1,
            grid=(2,),
            in_specs=[INSIDE] * 2
            + [INSIDE] * 4
            + [pl.BlockSpec((tile, 128), table)] * 2,
            out_specs=out_specs,
            scratch_shapes=scratch,
        ),
        out_shape=out_shape,
        compiler_params=pltpu.CompilerParams(vmem_limit_bytes=40 << 20),
        cost_estimate=pl.CostEstimate(
            flops=4 * TOK * DEPTH * 512, transcendentals=0, bytes_accessed=8 << 20
        ),
    )(meta, *sides, *parts, *tables)


def attend_pages(pair, mode, meta, q_ref, out_ref, kvt, saved, bias, parts):
    role = meta[0]
    factor = (1.0 / math.sqrt(128)) * math.log2(math.e)
    tall = lax.broadcasted_iota(jnp.int32, (PAGE, 128), 0)

    def one_page(index, carry):
        rows = pl.ds(pl.multiple_of(index * PAGE, PAGE), PAGE)
        page = jnp.bitwise_xor(role, 2 * (index // 4) + pair) * 4 + index % 4
        live = meta[17 + page]
        reach = meta[1 + page]
        stack = [
            jnp.concatenate(
                [
                    q_ref[rows, 256 * h : 256 * h + 128],
                    q_ref[rows, 256 * h + 128 : 256 * h + 256],
                ],
                axis=0,
            )
            for h in range(2)
        ]

        def run(first, opened, closed, covered, shade, count):
            def scan(chunk, tops, width, masked):
                base = pl.multiple_of((first + 2 * chunk) * PAGE, PAGE)
                result = []
                for h in range(2):
                    scores = lax.dot_general(
                        kvt[h, pl.ds(base, width * CHUNK), :],
                        stack[h],
                        (((1,), (1,)), ((), ())),
                        preferred_element_type=F32,
                    )
                    if masked:
                        scores = scores + bias[shade]
                    for i in range(width):
                        saved[h, chunk + i] = scores[CHUNK * i : CHUNK * i + CHUNK]
                    peak = jnp.max(scores.reshape(width * CHUNK // 8, 8, 256), axis=0)
                    result.append(jnp.maximum(tops[h], peak))
                return tuple(result)

            tops = (jnp.full((8, 256), NEG, F32),) * 2
            twice = (closed - opened) // 2
            tops = lax.fori_loop(
                0, twice, lambda i, t: scan(opened + 2 * i, t, 2, False), tops
            )
            tops = lax.fori_loop(
                opened + 2 * twice, closed, lambda i, t: scan(i, t, 1, False), tops
            )
            tops = scan(covered, tops, 1, True)
            tops = [jnp.max(top, axis=0, keepdims=True) for top in tops]

            def fold(chunk, state, width):
                result = []
                for h in range(2):
                    total, acc = state[h]
                    pieces, weights = [], []
                    for i in range(width):
                        expo = jnp.exp2((saved[h, chunk + i] - tops[h]) * factor)
                        total = total + jnp.sum(
                            expo.reshape(CHUNK // 8, 8, 256), axis=0
                        )
                        weights.append(expo.astype(BF))
                    for i in range(2 * width):
                        at = pl.multiple_of((first + 2 * chunk + i) * PAGE, PAGE)
                        pieces.append(kvt[2 + h, pl.ds(at, PAGE), :])
                    acc = acc + jnp.dot(
                        jnp.concatenate(pieces, axis=1),
                        jnp.concatenate(weights, axis=0),
                        preferred_element_type=F32,
                    )
                    result.append((total, acc))
                return tuple(result)

            state = ((jnp.zeros((8, 256), F32), jnp.zeros((128, 256), F32)),) * 2
            state = lax.fori_loop(0, count // 2, lambda i, s: fold(2 * i, s, 2), state)
            state = lax.fori_loop(
                count // 2 * 2, count, lambda i, s: fold(i, s, 1), state
            )
            return [
                (tops[h], jnp.sum(state[h][0], axis=0, keepdims=True), state[h][1])
                for h in range(2)
            ]

        def finish(h, total, acc):
            value = jnp.transpose(acc / total)
            for g in range(2):
                part = value[128 * g : 128 * g + 128]
                part = jnp.where(tall < live, part, 0.0)
                at_lane = 256 * h + 128 * g
                out_ref[rows, at_lane : at_lane + 128] = part.astype(BF)

        if mode == "halo":
            pages = jnp.maximum(reach - page, 0)
            count = (pages + 1) // 2
            peaks, totals, sums = parts

            @pl.when(count > 0)
            def _():
                result = run(QPAGES - 2 * count, 1, count, 0, 2 + pages % 2, count)
                for h in range(2):
                    top, total, acc = result[h]
                    before = peaks[index, h][:1]
                    higher = jnp.maximum(top, before)
                    fade = jnp.exp2((top - higher) * factor)
                    keep = jnp.exp2((before - higher) * factor)
                    total = total * fade + totals[index, h][:1] * keep
                    acc = acc * fade + sums[index, h] * keep
                    finish(h, total, acc)

            @pl.when(count == 0)
            def _():
                for h in range(2):
                    finish(h, totals[index, h][:1], sums[index, h])

            return carry

        offset = jnp.minimum(reach, page) if mode == "own" else reach
        full = offset // 2
        result = run(QPAGES + page - offset, 0, full, full, offset % 2, full + 1)
        for h in range(2):
            top, total, acc = result[h]
            if mode == "own":
                peaks, totals, sums = parts
                peaks[index, h] = jnp.broadcast_to(top, (8, 256))
                totals[index, h] = jnp.broadcast_to(total, (8, 256))
                sums[index, h] = acc
            else:
                finish(h, total, acc)
        return carry

    lax.fori_loop(0, 8, one_page, 0)


def fill_pages(role, sides, kvt):
    for p in range(4):
        block = jnp.bitwise_xor(role, 2 * (p % 2) + p // 2)
        source = slice((p % 2) * TOK, (p % 2) * TOK + TOK)
        for at, side in sides:
            rows = pl.ds(pl.multiple_of((block + at) * TOK, TOK), TOK)
            kvt[:, rows, :] = side[p // 2][:, source, :]


def fill_bias(bias):
    key = lax.broadcasted_iota(jnp.int32, (CHUNK, 256), 0)
    gap = key - lax.broadcasted_iota(jnp.int32, (CHUNK, 256), 1) % PAGE
    for i in range(2):
        bias[i] = jnp.where(gap <= i * PAGE, 0.0, NEG)
    bias[2] = jnp.zeros((CHUNK, 256), F32)
    bias[3] = jnp.where(key < PAGE, NEG, 0.0)


def whole_kernel(pair, meta, q_ref, own0, own1, halo0, halo1, out_ref, kvt, saved, bias):
    fill_pages(meta[0], ((0, (halo0, halo1)), (4, (own0, own1))), kvt)
    kvt[:, pl.ds(2 * QTOK, CHUNK), :] = jnp.zeros((4, CHUNK, 128), BF)
    fill_bias(bias)
    attend_pages(pair, "all", meta, q_ref, out_ref, kvt, saved, bias, None)


def own_kernel(pair, meta, q_ref, own0, own1, peaks, totals, sums, kvt, saved, bias):
    fill_pages(meta[0], ((4, (own0, own1)),), kvt)
    kvt[:, pl.ds(2 * QTOK, CHUNK), :] = jnp.zeros((4, CHUNK, 128), BF)
    fill_bias(bias)
    parts = (peaks, totals, sums)
    attend_pages(pair, "own", meta, q_ref, None, kvt, saved, bias, parts)


def halo_kernel(pair, meta, q_ref, halo0, halo1, peaks, totals, sums, out_ref, *scratch):
    kvt, saved, bias = scratch
    fill_pages(meta[0], ((0, (halo0, halo1)),), kvt)
    fill_bias(bias)
    parts = (peaks, totals, sums)
    attend_pages(pair, "halo", meta, q_ref, out_ref, kvt, saved, bias, parts)


def attend_call(kernel, pair, meta, operands, shapes):
    return pl.pallas_call(
        functools.partial(kernel, pair),
        grid_spec=pltpu.PrefetchScalarGridSpec(
            num_scalar_prefetch=1,
            grid=(),
            in_specs=[INSIDE] * len(operands),
            out_specs=[INSIDE] * len(shapes),
            scratch_shapes=[
                pltpu.VMEM((4, 2 * QTOK + CHUNK, 128), BF),
                pltpu.VMEM((2, 9, CHUNK, 256), F32),
                pltpu.VMEM((4, CHUNK, 256), F32),
            ],
        ),
        out_shape=shapes,
        compiler_params=pltpu.CompilerParams(vmem_limit_bytes=40 << 20),
        cost_estimate=pl.CostEstimate(
            flops=2 << 30, transcendentals=2 << 20, bytes_accessed=6 << 20
        ),
    )(meta, *operands)


ROWS = [jax.ShapeDtypeStruct((2 * TOK, 512), BF)]
STATE = [
    jax.ShapeDtypeStruct((8, 2, 8, 256), F32),
    jax.ShapeDtypeStruct((8, 2, 8, 256), F32),
    jax.ShapeDtypeStruct((8, 2, 128, 256), F32),
]


def attend(meta, queries, own, halo, pair):
    operands = (queries, *own, *halo)
    return attend_call(whole_kernel, pair, meta, operands, ROWS)[0]


def attend_own(meta, queries, own, pair):
    return attend_call(own_kernel, pair, meta, (queries, *own), STATE)


def attend_halo(meta, queries, halo, parts, pair):
    operands = (queries, *halo, *parts)
    return attend_call(halo_kernel, pair, meta, operands, ROWS)[0]


def pack_kernel(meta, *refs):
    keys, values, out_refs, kv = refs[:2], refs[2:4], refs[4:8], refs[8]
    role = meta[0]
    for p in range(4):
        block = jnp.bitwise_xor(role, 2 * (p % 2) + p // 2)
        rows = pl.ds(pl.multiple_of(block * TOK, TOK), TOK)
        source = slice((p % 2) * TOK, (p % 2) * TOK + TOK)
        kv[:2, rows, :] = keys[p // 2][:2, source, :]
        kv[2:, rows, :] = values[p // 2][:, source, :]
    tall = lax.broadcasted_iota(jnp.int32, (PAGE, 128), 0)
    for p in range(4):
        target = jnp.bitwise_xor(role, p)
        for slot in range(4):
            page = meta[33 + target * 4 + slot]
            live = meta[17 + page]
            rows = pl.ds(pl.multiple_of(page * PAGE, PAGE), PAGE)
            for part in range(4):
                block = jnp.where(tall < live, kv[part, rows, :].astype(F32), 0.0)
                lanes = slice(128 * part, 128 * part + 128)
                out_refs[p][PAGE * slot : PAGE * slot + PAGE, lanes] = block.astype(BF)


def pack(meta, keys, values):
    return pl.pallas_call(
        pack_kernel,
        grid_spec=pltpu.PrefetchScalarGridSpec(
            num_scalar_prefetch=1,
            grid=(),
            in_specs=[INSIDE] * 4,
            out_specs=[INSIDE] * 4,
            scratch_shapes=[pltpu.VMEM((4, QTOK, 128), BF)],
        ),
        out_shape=[jax.ShapeDtypeStruct((TOK, 512), BF)] * 4,
        compiler_params=pltpu.CompilerParams(vmem_limit_bytes=30 << 20),
        name="pack_pages",
    )(meta, *keys, *values)


def unpack_kernel(meta, *refs):
    in_refs, key_ref, value_ref = refs[:4], refs[4], refs[5]
    step = pl.program_id(0)
    for p in range(4):

        @pl.when(step == p)
        def _(p=p):
            key_ref[...] = in_refs[p][:, :256]
            value_ref[...] = in_refs[p][:, 256:]


def unpack(meta, received):
    whole = pl.BlockSpec((TOK, 512), lambda i, m: (0, 0))
    column = pl.BlockSpec((TOK, 256), lambda i, m: (0, jnp.bitwise_xor(m[0], i)))
    return pl.pallas_call(
        unpack_kernel,
        grid_spec=pltpu.PrefetchScalarGridSpec(
            num_scalar_prefetch=1,
            grid=(4,),
            in_specs=[whole] * 4,
            out_specs=[column] * 2,
        ),
        out_shape=[jax.ShapeDtypeStruct((TOK, 1024), BF)] * 2,
        compiler_params=pltpu.CompilerParams(vmem_limit_bytes=30 << 20),
        name="unpack_pages",
    )(meta, *received)


def fill_rows(meta, parts, weight, parity):
    for half in range(2):
        for d in range(4):
            flip = jnp.bitwise_xor(lax.rem(meta[49] + d, 4), meta[0])

            @pl.when(lax.rem(flip, 2) == parity)
            def _(half=half, d=d, flip=flip):
                weight[half, flip // 2] = parts[4 * half + d][...].reshape(512, 1024)


def pair_product(in_refs, weight, half):
    return jnp.dot(
        in_refs[0][:TOK], weight[half, 0], preferred_element_type=F32
    ) + jnp.dot(in_refs[1][...], weight[half, 1], preferred_element_type=F32)


def near_kernel(meta, *refs):
    in_refs, parts, out_ref, weight = refs[:2], refs[2:10], refs[10], refs[11]
    fill_rows(meta, parts, weight, 0)
    for half in range(2):
        out_ref[half] = pair_product(in_refs, weight, half)


def far_kernel(meta, *refs):
    in_refs, parts, partial, out_ref, weight = (
        refs[:2], refs[2:10], refs[10], refs[11], refs[12]
    )
    step = pl.program_id(0)

    @pl.when(step == 0)
    def _():
        fill_rows(meta, parts, weight, 1)

    for half in range(2):

        @pl.when(step == half)
        def _(half=half):
            total = partial[half] + pair_product(in_refs, weight, half)
            out_ref[...] = total.astype(BF)


def output_near(meta, pair, parts):
    return pl.pallas_call(
        near_kernel,
        grid_spec=pltpu.PrefetchScalarGridSpec(
            num_scalar_prefetch=1,
            grid=(),
            in_specs=[INSIDE] * 10,
            out_specs=INSIDE,
            scratch_shapes=[pltpu.VMEM((2, 2, 512, 1024), BF)],
        ),
        out_shape=jax.ShapeDtypeStruct((2, TOK, 1024), F32),
        compiler_params=pltpu.CompilerParams(vmem_limit_bytes=32 << 20),
        name="output_near",
    )(meta, *pair, *parts)


def output_far(meta, pair, parts, partial):
    return pl.pallas_call(
        far_kernel,
        grid_spec=pltpu.PrefetchScalarGridSpec(
            num_scalar_prefetch=1,
            grid=(2,),
            in_specs=[INSIDE] * 11,
            out_specs=pl.BlockSpec(
                (TOK, 1024), lambda i, m: (0, jnp.bitwise_xor(m[0] // 2, i))
            ),
            scratch_shapes=[pltpu.VMEM((2, 2, 512, 1024), BF)],
        ),
        out_shape=jax.ShapeDtypeStruct((TOK, DEPTH), BF),
        compiler_params=pltpu.CompilerParams(vmem_limit_bytes=32 << 20),
        name="output_far",
    )(meta, *pair, *parts, partial)


def page_sources(page_slots, core):
    other = swap(page_slots, "c")
    first = jnp.where(core == 0, page_slots, other)
    second = jnp.where(core == 0, other, page_slots)
    slots = jnp.stack([first, second])
    wanted = jnp.arange(8, dtype=jnp.int32)
    hit = slots[:, None, :] == wanted[None, :, None]
    found = jnp.sum(jnp.where(hit, wanted[None, None, :], 0), axis=2)
    return (found + jnp.array([[0], [8]], jnp.int32)).reshape(16)


def previous_quad(block):
    names = ("y", "zl", "x", "c", "zh")
    route = [(i, i + 4) for i in range(124)]
    return lax.ppermute(block, names, route)


def shards(hidden_in, norm_gain, w_qk, w_v, w_o, prompt_pages, last_fill, page_slots):
    core = lax.axis_index("c")
    role = core * 2 + lax.axis_index("zh")
    y, x = lax.axis_index("y"), lax.axis_index("x")
    quad = (y * 2 + lax.axis_index("zl")) * 4 + x

    here = jnp.stack([role, y, x]).astype(jnp.int32)

    slices = pl.pallas_call(
        slices_kernel,
        grid_spec=pltpu.PrefetchScalarGridSpec(
            num_scalar_prefetch=1,
            grid=(1,),
            in_specs=[
                pl.BlockSpec(block.shape, lambda i, m: (0, 0))
                for block in (w_qk, w_v, w_o)
            ],
            out_specs=INSIDE,
        ),
        out_shape=jax.ShapeDtypeStruct((8, 16, 2048), BF),
        name="role_slices",
    )(here, w_qk, w_v, w_o)
    level = lax.all_to_all(
        slices, ("zl", "c", "zh"), split_axis=0, concat_axis=0, tiled=True
    ).reshape(2, 64, 2048)
    kv_level, q_level, o_level = small(
        split_kernel, here, (level,), [(2, 64, 512), (2, 64, 512), (2, 64, 1024)]
    )
    kv_row = small(
        column_kernel, here, ring_pieces(kv_level, "y"), [(4, 2, 64, 512)]
    )[0]
    kv_parts = ring_pieces(kv_row, "x")
    q_row = small(arrange_kernel, here, ring_pieces(q_level, "x"), [(2, 4, 64, 512)])[0]
    q_parts = ring_pieces(q_row, "y")
    o_row = small(
        arrange_kernel, here, ring_pieces(o_level, "x"), [(2, 4, 64, 1024)]
    )[0]
    o_parts = ring_chain(o_row, "y")

    normed = normalize(after(hidden_in, slices), norm_gain)
    beside = swap(normed, "c")
    across = swap(after(normed, level), "zh")
    diagonal = swap(across, "c")

    offset, live = page_tables(prompt_pages, last_fill, quad * QPAGES)
    sources = page_sources(page_slots, core)
    meta = jnp.concatenate(
        [role[None], offset, live, sources, y[None], x[None]]
    ).astype(jnp.int32)
    tables = rotation_tables(offset)

    sides = ((normed, beside), (across, diagonal))
    keys, values, halo, queries = [], [], [], []
    metas = (meta, tick(meta))
    for pair in range(2):
        kvt, v = project(metas[pair], sides[pair], kv_parts, tables, pair, "kv")
        keys.append(kvt)
        values.append(v)
        halo.append(previous_quad(kvt))
        queries += project(meta, sides[pair], q_parts, tables, pair, "q")
    packed = pack(meta, keys, values)
    pages = [packed[0]]
    for flip in (1, 2, 3):
        pages.append(to_role(packed[flip], flip))

    parts = attend_own(meta, queries[1], keys, 1)
    far = attend_halo(meta, queries[1], halo, parts, 1)
    far = swap(far, "zh")
    near = attend(meta, queries[0], keys, halo, 0)
    o_parts = list(o_parts)
    for i in range(4):
        o_parts.append(swap(o_parts[i], "c"))
    partial = output_near(meta, (near, swap(near[TOK:], "c")), o_parts)
    diagonal_far = swap(far[TOK:], "c")
    attended = output_far(meta, (far, diagonal_far), o_parts, partial)
    key_cache, value_cache = unpack(meta, pages)
    return (
        attended,
        key_cache.reshape(4, PAGE, 1024),
        value_cache.reshape(4, PAGE, 1024),
    )


def solution(mesh):
    fine = Mesh(mesh.devices.reshape(SIZES), AXES)
    rows = P(AXES, None)
    in_specs = (rows, P(), rows, rows, rows, P(), P(), P(("y", "zl", "x", "c")))
    out_specs = (rows, P(AXES, None, None), P(AXES, None, None))
    return jax.shard_map(
        shards, mesh=fine, in_specs=in_specs, out_specs=out_specs, check_vma=False
    )
```
